256 devices in a mesh: tok: 64 (over z, y, core), rep: 4 (over x).
Axes of the slice: x: 4, y: 4, z: 8, core: 2. Of those that a mesh axis runs over, the one named last changes fastest.
Arguments:
- patches: bfloat16 [65536, 768], P(('tok', 'rep')), may hold values from -6 to 6
- patch_view: int32 [65536], P(('tok', 'rep')), may hold values from 0 to 511
- rays: bfloat16 [65536, 768], P(('tok', 'rep')), may hold values from -24 to 24
- ray_view: int32 [65536], P(('tok', 'rep')), may hold values from 0 to 511
- targets: float32 [3, 65536], P(None, ('tok', 'rep')), may hold values from -6 to 6
- camera: bfloat16 [512, 768], P('tok'), may hold values from -6 to 6
- slots_init: float32 [64, 768], replicated, may hold values from -6 to 6
- key_weight: bfloat16 [768, 768], P('tok'), may hold values from -0.875 to 0.875
- value_weight: bfloat16 [768, 768], P('tok'), may hold values from -0.4375 to 0.4375
- query_weight: bfloat16 [768, 768], P('tok'), may hold values from -0.21875 to 0.21875
- gru_input: bfloat16 [768, 2304], P('tok'), may hold values from -0.21875 to 0.21875
- gru_hidden: bfloat16 [768, 2304], P('tok'), may hold values from -0.21875 to 0.21875
- mix_query: bfloat16 [768, 768], P('tok'), may hold values from -0.875 to 0.875
- mix_key: bfloat16 [768, 768], P('tok'), may hold values from -0.21875 to 0.21875
- render_in: bfloat16 [768, 1536], P('tok'), may hold values from -0.21875 to 0.21875
- render_out: bfloat16 [3, 1536], P(None, 'tok'), may hold values from -0.15625 to 0.15625
Outputs:
- slots_out: float32 [64, 768], replicated
- colour: float32 [3, 65536], P(None, ('tok', 'rep'))
- loss: float32 [], replicated
- grad_render_in: float32 [768, 1536], P('tok')
- grad_render_out: float32 [3, 1536], replicated
The draws below stay inside these ranges and needn't reach their ends.
All inputs are finite; a program needn't handle non-finite values.
Results may differ from the reference program's by a relative error of at most 0.019.
Values may be sent and summed in bfloat16 or wider, within the bound.
A program may use at most 128 MiB of HBM per device.

```python
import jax
import jax.numpy as jnp
from jax import lax

D = 768
H = 1536
SLOTS = 64
ITERS = 3
VIEWS = 512
TOKENS = 65536
RAYS = 65536


def set_ends(entries, key, smallest, largest):
    longest = entries.shape.index(max(entries.shape))
    spots = []
    for shift in (0, 1):
        where = [jax.random.randint(jax.random.fold_in(key, axis), (), 0, length) for axis, length in enumerate(entries.shape)]
        where[longest] = (where[longest] + shift) % entries.shape[longest]
        spots.append(tuple(where))
    return entries.at[spots[0]].set(smallest).at[spots[1]].set(largest)


def raised(array, key, source, target, blocks, factor):
    def block_of(dim):
        return (jnp.arange(array.shape[dim]) // (array.shape[dim] // blocks)).reshape((-1,) + (1,) * (array.ndim - 1 - dim))

    near = jax.random.permutation(key, blocks)[block_of(target)]
    far = (block_of(target) + blocks // 2) % blocks
    return jnp.where((block_of(source) == near) | (block_of(source) == far), factor * array, array)


def level_of(stream_key, dims, split, least, largest):
    def one(position, parts):
        draws = jax.random.uniform(jax.random.fold_in(jax.random.fold_in(stream_key, 6), position), (parts,), jnp.float32, least / len(split), largest / len(split))
        return jnp.repeat(jnp.exp(draws), dims[position] // parts).reshape((-1,) + (1,) * (len(dims) - position - 1))

    factor_of = one(*split[0])
    for cut in split[1:]:
        factor_of = factor_of * one(*cut)
    return factor_of


def gaussian(rng, extent, scale, limit, pieces=(), dtype=jnp.bfloat16):
    entries = scale * jax.random.normal(rng, extent, jnp.float32)
    if pieces:
        entries = entries * level_of(rng, extent, pieces, -0.22, 0.18)
    return jnp.clip(entries, -limit, limit).astype(dtype)


def heavy_noise(stream_key, dims, scale, most, split, heavy, kind=jnp.bfloat16):
    drawn = scale * jax.random.normal(stream_key, dims, jnp.float32)
    if split:
        drawn = drawn * level_of(stream_key, dims, split, -0.22, 0.18)
    return jnp.clip(raised(drawn, jax.random.fold_in(stream_key, 3), *heavy), -most, most).astype(kind)


def setup_inputs(seed: int = 0) -> dict:
    arg_keys = jax.random.split(jax.random.key(seed), 17)
    return {
        "patches": gaussian(arg_keys[0], (TOKENS, D), 1.0, 6.0, ((0, 256),)),
        "patch_view": set_ends(jax.random.randint(arg_keys[1], (TOKENS,), 0, VIEWS), jax.random.fold_in(arg_keys[1], 1), 0, VIEWS - 1).astype(jnp.int32),
        "rays": heavy_noise(arg_keys[2], (RAYS, D), 1.0, 24.0, ((0, 256),), (0, 1, 256, 6.0)),
        "ray_view": set_ends(jax.random.randint(arg_keys[3], (RAYS,), 0, VIEWS), jax.random.fold_in(arg_keys[3], 1), 0, VIEWS - 1).astype(jnp.int32),
        "targets": gaussian(arg_keys[4], (3, RAYS), 1.0, 6.0, ((1, 256),), jnp.float32),
        "camera": gaussian(arg_keys[5], (VIEWS, D), 1.0, 6.0, ((0, 64),)),
        "slots_init": gaussian(arg_keys[6], (SLOTS, D), 1.0, 6.0, (), jnp.float32),
        "key_weight": gaussian(arg_keys[7], (D, D), (D // 16) ** -0.5, 0.875, ((0, 64),)),
        "value_weight": gaussian(arg_keys[8], (D, D), (D // 4) ** -0.5, 0.4375, ((0, 64),)),
        "query_weight": gaussian(arg_keys[9], (D, D), D ** -0.5, 0.21875, ((0, 64),)),
        "gru_input": gaussian(arg_keys[10], (D, 3 * D), D ** -0.5, 0.21875, ((0, 64),)),
        "gru_hidden": gaussian(arg_keys[11], (D, 3 * D), D ** -0.5, 0.21875, ((0, 64),)),
        "mix_query": gaussian(arg_keys[12], (D, D), (D // 16) ** -0.5, 0.875, ((0, 64),)),
        "mix_key": gaussian(arg_keys[13], (D, D), D ** -0.5, 0.21875, ((0, 64),)),
        "render_in": gaussian(arg_keys[14], (D, H), D ** -0.5, 0.21875, ((0, 64),)),
        "render_out": gaussian(arg_keys[15], (3, H), H ** -0.5, 0.15625, ((1, 64),)),
    }


EPSILON = 1e-05
ATTN_FLOOR = 1e-08

def normalize(values):
    mean = lax.optimization_barrier(jnp.mean(values, axis=-1, keepdims=True))
    centred = values - mean
    spread = lax.optimization_barrier(jnp.mean(centred * centred, axis=-1, keepdims=True))
    return centred * lax.rsqrt(spread + EPSILON)

def slot_update(slots, update, gru_input, gru_hidden):
    width = slots.shape[1]
    from_update = jnp.dot(update.astype(jnp.bfloat16), gru_input, preferred_element_type=jnp.float32)
    from_state = jnp.dot(slots.astype(jnp.bfloat16), gru_hidden, preferred_element_type=jnp.float32)
    reset = jax.nn.sigmoid(from_update[:, :width] + from_state[:, :width])
    blend = jax.nn.sigmoid(from_update[:, width:2 * width] + from_state[:, width:2 * width])
    candidate = jnp.tanh(from_update[:, 2 * width:] + reset * from_state[:, 2 * width:])
    return (1.0 - blend) * candidate + blend * slots

def reference(patches, patch_view, rays, ray_view, targets, camera, slots_init, key_weight, value_weight, query_weight, gru_input, gru_hidden, mix_query, mix_key, render_in, render_out):
    scale = D ** (-0.5)
    patch_in = patches.astype(jnp.float32) + camera[patch_view].astype(jnp.float32)
    patch_x = normalize(patch_in).astype(jnp.bfloat16)
    keys = jnp.dot(patch_x, key_weight, preferred_element_type=jnp.float32).astype(jnp.bfloat16)
    values = jnp.dot(patch_x, value_weight, preferred_element_type=jnp.float32).astype(jnp.bfloat16)
    slots = slots_init
    for step in range(ITERS):
        query = (jnp.dot(normalize(slots).astype(jnp.bfloat16), query_weight, preferred_element_type=jnp.float32) * scale).astype(jnp.bfloat16)
        logits = jnp.dot(keys, query.T, preferred_element_type=jnp.float32)
        attn = jax.nn.softmax(logits, axis=1) + ATTN_FLOOR
        numer = jnp.dot(attn.astype(jnp.bfloat16).T, values, preferred_element_type=jnp.float32)
        denom = lax.optimization_barrier(jnp.sum(attn, axis=0))
        slots = slot_update(slots, numer / denom[:, None], gru_input, gru_hidden)
    slots_low = slots.astype(jnp.bfloat16)
    ray_in = rays.astype(jnp.float32) + camera[ray_view].astype(jnp.float32)
    ray_x = ray_in.astype(jnp.bfloat16)
    ray_query = (jnp.dot(ray_x, mix_query, preferred_element_type=jnp.float32) * scale).astype(jnp.bfloat16)
    slot_keys = jnp.dot(slots_low, mix_key, preferred_element_type=jnp.float32).astype(jnp.bfloat16)
    mix = jax.nn.softmax(jnp.dot(ray_query, slot_keys.T, preferred_element_type=jnp.float32), axis=1).astype(jnp.bfloat16)
    joined = (jnp.dot(mix, slots_low, preferred_element_type=jnp.float32) + ray_in).astype(jnp.bfloat16)
    pre = jnp.dot(joined, render_in, preferred_element_type=jnp.float32)
    hidden = jax.nn.silu(pre).astype(jnp.bfloat16)
    colour = lax.dot_general(render_out, hidden, (((1,), (1,)), ((), ())), preferred_element_type=jnp.float32)
    error = colour - targets
    loss = jnp.sum(error * error) / (3.0 * RAYS)
    dcol = (error * (2.0 / jnp.sqrt(jnp.float32(3.0 * RAYS)))).astype(jnp.bfloat16)
    grad_render_out = jnp.dot(dcol, hidden, preferred_element_type=jnp.float32)
    dhidden = jnp.dot(dcol.T, render_out, preferred_element_type=jnp.float32)
    sig = jax.nn.sigmoid(pre)
    dpre = (dhidden * (sig + pre * sig * (1.0 - sig))).astype(jnp.bfloat16)
    grad_render_in = lax.dot_general(joined, dpre, (((0,), (0,)), ((), ())), preferred_element_type=jnp.float32)
    return (slots, colour, loss, grad_render_in, grad_render_out)
```

```python
import functools

import jax
import jax.numpy as jnp
from jax import lax
from jax.experimental import pallas as pl
from jax.experimental.pallas import tpu as pltpu
from jax.sharding import Mesh
from jax.sharding import PartitionSpec as P

ITERS = 3
EPSILON = 1e-05
ATTN_FLOOR = 1e-08
NZ, NY, NC, NX = 8, 4, 2, 4
BF = jnp.bfloat16
F32 = jnp.float32

OFF = (0, 1536, 3072, 7680)
LEN = (1536, 1536, 4608, 2560)
NB = 4


def dot(a, b, ca=1, cb=0):
    return lax.dot_general(a, b, (((ca,), (cb,)), ((), ())), preferred_element_type=F32)


def normalize(values):
    mean = jnp.mean(values, axis=-1, keepdims=True)
    centred = values - mean
    spread = jnp.mean(centred * centred, axis=-1, keepdims=True)
    return centred * lax.rsqrt(spread + EPSILON)


def onehot(mask):
    return mask.astype(F32).astype(BF)


def softmax0(logits):
    top = jnp.max(logits, axis=0, keepdims=True)
    e = jnp.exp(logits - top)
    return e / jnp.sum(e, axis=0, keepdims=True)


def rows(start, size):
    return pl.ds(pl.multiple_of(start, 16), size)


def lanes(start, size):
    return pl.ds(pl.multiple_of(start, 128), size)


def kernel(
    pview, rview, patches, rays, targets, slots_init, packed, camera,
    slots_out, colour_out, loss_out, gin_out, gro_out,
    cy0, cy1, cy2, cy3, f0, f1, f2, f3, sg0, sg1, sg2, sg3, camsg, camcy, camf,
    px, rin, rx, ro, state, tsend, trecv, tysend, tyrecv, tzsend, tzrecv,
    psend, precv, ssend, srecv, dcol8, small, smrecv_cx, smrecv_y, smrecv_z, smy, smz,
    jt, gown, gcs, gcr, gxs, gxr, gzs, gzr, gys, gyr, gfs, gfr,
    cy_s, cy_r, z_s, z_r, x_s, x_r, c_s, c_r, it_s, it_r, gr_s, gr_r,
):
    z, y, c, x = (lax.axis_index(a) for a in ("z", "y", "c", "x"))
    cyb, full, stage = (cy0, cy1, cy2, cy3), (f0, f1, f2, f3), (sg0, sg1, sg2, sg3)
    width = patches.shape[1]
    scale = width ** (-0.5)
    pending = []

    def send(src, dst, ssem, rsem, **where):
        cp = pltpu.make_async_remote_copy(
            src_ref=src, dst_ref=dst, send_sem=ssem, recv_sem=rsem,
            device_id=where, device_id_type=pl.DeviceIdType.MESH,
        )
        cp.start()
        pending.append(cp)
        return cp

    def yc_peers():
        return [(dy, dc) for dy in range(NY) for dc in range(NC) if dy or dc]

    def cx_peers():
        return [(dc, dx) for dc in range(NC) for dx in range(NX) if dc or dx]

    def flip(dc):
        return 1 - c if dc else c

    barrier = pltpu.get_barrier_semaphore()
    met = 0
    for dy, dc in yc_peers():
        pl.semaphore_signal(barrier, inc=1, device_id={"y": lax.rem(y + dy, NY), "c": flip(dc)}, device_id_type=pl.DeviceIdType.MESH)
        met += 1
    for dc, dx in cx_peers():
        if dx:
            pl.semaphore_signal(barrier, inc=1, device_id={"x": lax.rem(x + dx, NX), "c": flip(dc)}, device_id_type=pl.DeviceIdType.MESH)
            met += 1
    for dz in range(1, NZ):
        pl.semaphore_signal(barrier, inc=1, device_id={"z": lax.rem(z + dz, NZ)}, device_id_type=pl.DeviceIdType.MESH)
        met += 1
    pl.semaphore_wait(barrier, met)

    me_yc = y * 2 + c

    def start_yc(src, buf, slot):
        buf[rows(me_yc * 16, 16), :] = src[...]
        out = []
        for k, (dy, dc) in enumerate(yc_peers()):
            out.append(send(src, buf.at[rows(me_yc * 16, 16)], cy_s.at[slot, k], cy_r.at[slot, k],
                            y=lax.rem(y + dy, NY), c=flip(dc)))
        return out

    def start_bundle(b):
        w = LEN[b] // NX
        stage[b][...] = packed[:, lanes(OFF[b] + x * w, w)]
        return start_yc(stage[b], cyb[b], b)

    def compact(shards, real, first, count):
        r = lax.broadcasted_iota(jnp.int32, (count, 128), 0) + first
        k = lax.broadcasted_iota(jnp.int32, (count, 128), 1)
        lane = k % 16
        mask = (lane < real) & (r == (k // 16) * real + lane)
        return dot(onehot(mask), shards).astype(BF)

    def piece(b, zz):
        w = LEN[b] // NX
        return full[b].at[rows(zz * 96 + c * 48, 48), lanes(x * w, w)]

    def start_z(b, arrived):
        for cp in arrived:
            cp.wait()
        w = LEN[b] // NX
        full[b][rows(z * 96 + c * 48, 48), lanes(x * w, w)] = compact(cyb[b][...], 12, c * 48, 48)
        return [
            send(piece(b, z), piece(b, z), z_s.at[b, d], z_r.at[b, d], z=lax.rem(z + d, NZ))
            for d in range(1, NZ)
        ]

    def forward_x(b, ref, d):
        return [
            send(ref, ref, x_s.at[b, dx, d], x_r.at[b, dx, d], x=lax.rem(x + dx, NX))
            for dx in range(1, NX)
        ]

    def start_x(b, arriving):
        out = forward_x(b, piece(b, z), 0)
        for d in range(1, NZ):
            arriving[d - 1].wait()
            out += forward_x(b, piece(b, lax.rem(z - d + NZ, NZ)), d)
        return out

    def swap_core(b, arriving):
        for cp in arriving:
            cp.wait()
        cps = []
        for zz in range(NZ):
            ref = full[b].at[rows(zz * 96 + c * 48, 48)]
            cps.append(send(ref, ref, c_s.at[b, zz], c_r.at[b, zz], c=1 - c))
        return cps

    def done(cps):
        for cp in cps:
            cp.wait()

    cy_b0 = start_bundle(0)
    camsg[...] = camera[...]
    cy_cam = start_yc(camsg, camcy, 4)
    n0 = normalize(slots_init[...]).astype(BF)
    z_b0 = start_z(0, cy_b0)
    done(cy_cam)
    half = width // 2
    camf[rows(z * 64 + x * 16, 16), lanes(c * half, half)] = compact(camcy[:, lanes(c * half, half)], 8, x * 16, 16)

    def cam_piece(zz):
        return camf.at[rows(zz * 64 + x * 16, 16), lanes(c * half, half)]

    z_cam = [
        send(cam_piece(z), cam_piece(z), z_s.at[4, d], z_r.at[4, d], z=lax.rem(z + d, NZ))
        for d in range(1, NZ)
    ]
    cy_b2 = start_bundle(2)
    cy_b1 = start_bundle(1)
    x_cam = forward_x(4, cam_piece(z), 0)
    for d in range(1, NZ):
        z_cam[d - 1].wait()
        x_cam += forward_x(4, cam_piece(lax.rem(z - d + NZ, NZ)), d)
    x_b0 = start_x(0, z_b0)
    z_b2 = start_z(2, cy_b2)
    z_b1 = start_z(1, cy_b1)
    done(x_cam)
    cam_half = camf.at[:, lanes(c * half, half)]
    done([send(cam_half, cam_half, c_s.at[4, 0], c_r.at[4, 0], c=1 - c)])

    def lookup(view):
        v = lax.broadcasted_iota(jnp.int32, (camf.shape[0], view.shape[1]), 0)
        return dot(onehot(v == view[...]), camf[...], 0, 0)

    px[...] = normalize(patches[...].astype(F32) + lookup(pview)).astype(BF)
    rin[...] = rays[...].astype(F32) + lookup(rview)
    rx[...] = rin[...].astype(BF)
    done(swap_core(0, x_b0))

    def slot_projection(normed):
        query = (dot(normed, f0[:, 0:width]) * scale).astype(BF)
        return dot(query, f0[:, width : 2 * width], 1, 1).astype(BF)

    group = c * NX + x
    mine = pl.ds(pl.multiple_of(group * 8, 8), 8)
    state[...] = slots_init[mine, :]
    proj = slot_projection(n0)
    x_b1 = x_b2 = x_b3 = cy_b3 = z_b3 = c_b3 = None

    def group_rows(buf, t):
        return jnp.concatenate([buf[t, g].astype(F32) for g in range(8)], axis=0)

    def share(t, value):
        psend[t] = value
        precv[t, group] = value
        return [
            send(psend.at[t], precv.at[t, group], it_s.at[t, 24 + k], it_r.at[t, 24 + k],
                 c=flip(dc), x=lax.rem(x + dx, NX))
            for k, (dc, dx) in enumerate(cx_peers())
        ]

    for t in range(ITERS):
        attn = softmax0(dot(proj, px[...], 1, 1)) + ATTN_FLOOR
        total = dot(attn.astype(BF), px[...])
        denom = jnp.sum(attn, axis=1, keepdims=True)
        for g in range(8):
            tsend[t, g, :, 0:width] = total[8 * g : 8 * g + 8].astype(BF)
            tsend[t, g, :, width : width + 128] = jnp.broadcast_to(denom[8 * g : 8 * g + 8], (8, 128)).astype(BF)
        cps = []
        for k, (dc, dx) in enumerate(cx_peers()):
            cc, xx = flip(dc), lax.rem(x + dx, NX)
            cps.append(send(tsend.at[t, cc * NX + xx], trecv.at[t, k], it_s.at[t, k], it_r.at[t, k], c=cc, x=xx))
        if t == 0:
            x_b1 = start_x(1, z_b1)
            x_b2 = start_x(2, z_b2)
            cy_b3 = start_bundle(3)
        if t == 1:
            x_b3 = start_x(3, z_b3)
        if t == 2:
            c_b3 = swap_core(3, x_b3)
        acc = tsend[t, group].astype(F32)
        for k, cp in enumerate(cps):
            cp.wait()
            acc += trecv[t, k].astype(F32)
        tysend[t] = acc.astype(BF)
        cps = [
            send(tysend.at[t], tyrecv.at[t, d], it_s.at[t, 8 + d], it_r.at[t, 8 + d], y=lax.rem(y + d, NY))
            for d in range(1, NY)
        ]
        for cp in cps:
            cp.wait()
        acc = ordered(tyrecv, tysend, t, y, NY)
        tzsend[t] = acc.astype(BF)
        cps = [
            send(tzsend.at[t], tzrecv.at[t, d], it_s.at[t, 12 + d], it_r.at[t, 12 + d], z=lax.rem(z + d, NZ))
            for d in range(1, NZ)
        ]
        if t == 0:
            c_b1 = swap_core(1, x_b1)
            c_b2 = swap_core(2, x_b2)
            z_b3 = start_z(3, cy_b3)
        for cp in cps:
            cp.wait()
        acc = ordered(tzrecv, tzsend, t, z, NZ)
        if t == 0:
            done(c_b1)
            done(c_b2)
        mean_x = (acc[:, 0:width] / acc[:, width : width + 1]).astype(BF)
        update = dot(mean_x, f1[:, 0:width]).astype(BF)
        slots = state[...]
        a = dot(update, f2[:, 0 : 3 * width])
        b = dot(slots.astype(BF), f2[:, 3 * width : 6 * width])
        reset = jax.nn.sigmoid(a[:, 0:width] + b[:, 0:width])
        blend = jax.nn.sigmoid(a[:, width : 2 * width] + b[:, width : 2 * width])
        cand = jnp.tanh(a[:, 2 * width :] + reset * b[:, 2 * width :])
        slots = (1.0 - blend) * cand + blend * slots
        state[...] = slots
        if t + 1 < ITERS:
            cps = share(t, slot_projection(normalize(slots).astype(BF)))
            done(cps)
            proj = group_rows(precv, t).astype(BF)

    t = ITERS - 1
    ssend[...] = slots
    srecv[mine, :] = slots
    s_cps = [
        send(ssend, srecv.at[mine], gr_s.at[0, k], gr_r.at[0, k], c=flip(dc), x=lax.rem(x + dx, NX))
        for k, (dc, dx) in enumerate(cx_peers())
    ]
    done(c_b3)
    slot_keys = dot(slots.astype(BF), f1[:, width : 2 * width]).astype(BF)
    r_cps = share(t, (dot(slot_keys, f3[:, 0:width], 1, 1) * scale).astype(BF))
    r = lax.broadcasted_iota(jnp.int32, (width, 1), 0)
    hid = 2 * r - r % 12
    unit = lax.broadcasted_iota(jnp.int32, (width, 2 * width), 1)
    ro[...] = (
        dot(f3[:, 3 * width : 3 * width + 128], onehot(unit == hid), 0, 0)
        + dot(f3[:, 3 * width + 128 : 3 * width + 256], onehot(unit == hid + 12), 0, 0)
    )[0:8].astype(BF)
    done(s_cps)
    done(r_cps)
    slots_all = srecv[...]
    slots_out[...] = slots_all
    low = slots_all.astype(BF)
    mix = softmax0(dot(group_rows(precv, t).astype(BF), rx[...], 1, 1)).astype(BF)
    joined = (dot(mix, low, 0, 0) + rin[...]).astype(BF)
    pre = dot(joined, f3[:, width : 3 * width])
    sig = jax.nn.sigmoid(pre)
    hidden = (pre * sig).astype(BF)
    colour = dot(ro[...], hidden, 1, 1)[0:3]
    colour_out[...] = colour
    error = colour - targets[...]
    rays_total = rin.shape[0] * NZ * NY * NC * NX
    dcol8[...] = jnp.zeros_like(dcol8)
    dcol8[0:3, :] = error * (2.0 / jnp.sqrt(jnp.float32(3.0 * rays_total)))
    dcol = dcol8[...].astype(BF)
    dpre = (dot(dcol, ro[...], 0, 0) * (sig + pre * sig * (1.0 - sig))).astype(BF)
    gro = dot(dcol, hidden)
    squared = jnp.sum(jnp.sum(error * error, axis=1, keepdims=True), axis=0, keepdims=True)

    turned = jnp.transpose(joined.astype(F32)).astype(BF)
    for zz in range(NZ):
        for h in range(NC):
            jt[384 * h + 48 * zz : 384 * h + 48 * zz + 48, :] = turned[96 * zz + 48 * h : 96 * zz + 48 * h + 48]
    gcs[...] = dot(jt[rows(384 * (1 - c), 384), :], dpre).astype(BF)
    g_c = send(gcs, gcr, gr_s.at[1, 0], gr_r.at[1, 0], c=1 - c)
    small[...] = jnp.zeros_like(small)
    small[0:3, :] = gro[0:3, 0:width]
    small[3:6, :] = gro[0:3, width:]
    small[6:7, :] = jnp.broadcast_to(squared, (1, width))
    sm_cps = [
        send(small, smrecv_cx.at[group], gr_s.at[2, k], gr_r.at[2, k], c=flip(dc), x=lax.rem(x + dx, NX))
        for k, (dc, dx) in enumerate(cx_peers())
    ]
    smrecv_cx[group] = small[...]
    gown[...] = dot(jt[rows(384 * c, 384), :], dpre)
    g_c.wait()
    gown[...] += gcr[...].astype(F32)
    gxs[...] = gown[...].astype(BF)
    quarter = 2 * width // NX
    gx = [
        send(gxs.at[:, lanes(lax.rem(x + d, NX) * quarter, quarter)], gxr.at[d], gr_s.at[3, d], gr_r.at[3, d], x=lax.rem(x + d, NX))
        for d in range(1, NX)
    ]
    done(sm_cps)
    acc_s = sum_of(smrecv_cx, 8)
    smy[...] = acc_s
    smrecv_y[y] = acc_s
    sm_cps = [
        send(smy, smrecv_y.at[y], gr_s.at[4, d], gr_r.at[4, d], y=lax.rem(y + d, NY)) for d in range(1, NY)
    ]
    done(sm_cps)
    acc_s = sum_of(smrecv_y, NY)
    smz[...] = acc_s
    smrecv_z[z] = acc_s
    sm_cps = [
        send(smz, smrecv_z.at[z], gr_s.at[5, d], gr_r.at[5, d], z=lax.rem(z + d, NZ)) for d in range(1, NZ)
    ]
    acc_g = gown[:, lanes(x * quarter, quarter)]
    for d, cp in enumerate(gx):
        cp.wait()
        acc_g += gxr[d + 1].astype(F32)
    gzs[...] = acc_g.astype(BF)
    gz = [
        send(gzs.at[rows(lax.rem(z + d, NZ) * 48, 48)], gzr.at[d], gr_s.at[6, d], gr_r.at[6, d], z=lax.rem(z + d, NZ))
        for d in range(1, NZ)
    ]
    done(sm_cps)
    acc_s = sum_of(smrecv_z, NZ)
    gro_out[:, 0:width] = acc_s[0:3]
    gro_out[:, width:] = acc_s[3:6]
    loss_out[...] = acc_s[6:7, 0:1] / (3.0 * rays_total)
    acc_g = gzs[rows(z * 48, 48), :].astype(F32)
    for d, cp in enumerate(gz):
        cp.wait()
        acc_g += gzr[d + 1].astype(F32)
    gys[...] = acc_g
    for d in range(1, NY):
        to = lax.rem(y + d, NY)

        @pl.when(to // 2 == c)
        def _():
            pltpu.make_async_remote_copy(
                src_ref=gys, dst_ref=gyr.at[d], send_sem=gr_s.at[7, d], recv_sem=gr_r.at[7, d],
                device_id={"y": to}, device_id_type=pl.DeviceIdType.MESH,
            ).start()

    def final(k, dc, dx):
        return pltpu.make_async_remote_copy(
            src_ref=gfs, dst_ref=gfr.at[x], send_sem=gr_s.at[8, k], recv_sem=gr_r.at[8, dx],
            device_id={"c": flip(dc), "x": lax.rem(x + dx, NX)}, device_id_type=pl.DeviceIdType.MESH,
        )

    @pl.when(y // 2 == c)
    def _():
        acc = gys[...]
        for d in range(1, NY):
            pltpu.make_async_remote_copy(
                src_ref=gys, dst_ref=gyr.at[d], send_sem=gr_s.at[7, d], recv_sem=gr_r.at[7, d],
                device_id={"y": lax.rem(y + d, NY)}, device_id_type=pl.DeviceIdType.MESH,
            ).wait_recv()
            acc += gyr[d]
        part = jnp.where(y % 2 == 0, acc[0:24], acc[24:48])
        gfs[...] = part
        gfr[x] = part
        for k, (dc, dx) in enumerate(cx_peers()):
            final(k, dc, dx).start()

    for d in range(1, NY):
        to = lax.rem(y + d, NY)

        @pl.when(to // 2 == c)
        def _():
            pltpu.make_async_remote_copy(
                src_ref=gys, dst_ref=gyr.at[d], send_sem=gr_s.at[7, d], recv_sem=gr_r.at[7, d],
                device_id={"y": to}, device_id_type=pl.DeviceIdType.MESH,
            ).wait_send()

    @pl.when(y // 2 != c)
    def _():
        final(0, 0, 0).wait_recv()

    for dx in range(1, NX):
        final(0, 0, dx).wait_recv()
    for xx in range(NX):
        blk = gfr[xx]
        gin_out[:, quarter * xx : quarter * xx + quarter] = jnp.where(c == 0, blk[0:12], blk[12:24])

    @pl.when(y // 2 == c)
    def _():
        for k, (dc, dx) in enumerate(cx_peers()):
            final(k, dc, dx).wait_send()


def sum_of(buf, n):
    acc = buf[0]
    for j in range(1, n):
        acc += buf[j]
    return acc


def ordered(recv, own, t, me, n):
    acc = None
    for j in range(n):
        d = lax.rem(me - j + n, n)
        val = jnp.where(d == 0, own[t].astype(F32), recv[t, d].astype(F32))
        acc = val if acc is None else acc + val
    return acc


def on_device(
    patches, patch_view, rays, ray_view, targets, camera, slots_init, key_weight, value_weight,
    query_weight, gru_input, gru_hidden, mix_query, mix_key, render_in, render_out,
):
    n, width = patches.shape
    units = jnp.pad(render_out.T, ((0, 0), (0, 125)))
    pair = jnp.concatenate([units[0:12], units[12:24]], axis=1)
    packed = jnp.concatenate(
        [query_weight, key_weight, value_weight, mix_key, gru_input, gru_hidden, mix_query, render_in, pair], axis=1
    )
    packed = jnp.pad(packed, ((0, 4), (0, 0)))
    cam = jnp.pad(camera, ((0, 8), (0, 0)))
    V, S = pltpu.VMEM, pltpu.SemaphoreType.DMA
    vm = pl.BlockSpec(memory_space=pltpu.VMEM)
    scratch = (
        [V((128, L // NX), BF) for L in LEN]
        + [V((width, L), BF) for L in LEN]
        + [V((16, L // NX), BF) for L in LEN]
        + [
            V((16, width), BF), V((128, width), BF), V((512, width), BF),
            V((n, width), BF), V((n, width), F32), V((n, width), BF), V((8, 2 * width), BF), V((8, width), F32),
            V((3, 8, 8, width + 128), BF), V((3, 8, 8, width + 128), BF),
            V((3, 8, width + 128), BF), V((3, NY, 8, width + 128), BF),
            V((3, 8, width + 128), BF), V((3, NZ, 8, width + 128), BF),
            V((3, 8, width), BF), V((3, 8, 8, width), BF), V((8, width), F32), V((64, width), F32),
            V((8, n), F32), V((8, width), F32), V((8, 8, width), F32), V((NY, 8, width), F32), V((NZ, 8, width), F32),
            V((8, width), F32), V((8, width), F32),
            V((width, n), BF), V((384, 2 * width), F32), V((384, 2 * width), BF), V((384, 2 * width), BF),
            V((384, 2 * width), BF), V((NX, 384, width // 2), BF), V((384, width // 2), BF), V((NZ, 48, width // 2), BF),
            V((48, width // 2), F32), V((NY, 48, width // 2), F32), V((24, width // 2), F32), V((NX, 24, width // 2), F32),
            S((5, 7)), S((5, 7)), S((5, 8)), S((5, 8)), S((5, 4, 8)), S((5, 4, 8)), S((5, 8)), S((5, 8)),
            S((3, 32)), S((3, 32)), S((9, 8)), S((9, 8)),
        ]
    )
    out = pl.pallas_call(
        kernel,
        out_shape=[
            jax.ShapeDtypeStruct((64, width), F32),
            jax.ShapeDtypeStruct((3, n), F32),
            jax.ShapeDtypeStruct((1, 1), F32),
            jax.ShapeDtypeStruct((12, 2 * width), F32),
            jax.ShapeDtypeStruct((3, 2 * width), F32),
        ],
        in_specs=[vm] * 8,
        out_specs=[vm] * 5,
        scratch_shapes=scratch,
        compiler_params=pltpu.CompilerParams(collective_id=0, has_side_effects=True, vmem_limit_bytes=60 << 20),
    )(patch_view[None], ray_view[None], patches, rays, targets, slots_init, packed, cam)
    slots, colour, loss, gin, gro = out
    return slots, colour, loss[0, 0], gin, gro


def solution(mesh):
    torus = Mesh(mesh.devices.reshape(NZ, NY, NC, NX), ("z", "y", "c", "x"))
    tok, every = ("z", "y", "c"), ("z", "y", "c", "x")
    w = P(tok, None)
    return jax.shard_map(
        on_device,
        mesh=torus,
        in_specs=(
            P(every, None), P(every), P(every, None), P(every), P(None, every), w, P(),
            w, w, w, w, w, w, w, w, P(None, tok),
        ),
        out_specs=(P(), P(None, every), P(), w, P()),
        check_vma=False,
    )
```

```python
import functools

import jax
import jax.numpy as jnp
from jax import lax
from jax.experimental import pallas as pl
from jax.experimental.pallas import tpu as pltpu
from jax.sharding import Mesh
from jax.sharding import PartitionSpec as P

ITERS = 3
EPSILON = 1e-05
ATTN_FLOOR = 1e-08
NZ, NY, NC, NX = 8, 4, 2, 4
BF = jnp.bfloat16
F32 = jnp.float32

OFF = (0, 1536, 3072, 7680)
LEN = (1536, 1536, 4608, 2560)
NB = 4


def dot(a, b, ca=1, cb=0):
    return lax.dot_general(a, b, (((ca,), (cb,)), ((), ())), preferred_element_type=F32)


def normalize(values):
    mean = jnp.mean(values, axis=-1, keepdims=True)
    centred = values - mean
    spread = jnp.mean(centred * centred, axis=-1, keepdims=True)
    return centred * lax.rsqrt(spread + EPSILON)


def onehot(mask):
    return mask.astype(F32).astype(BF)


def softmax0(logits):
    top = jnp.max(logits, axis=0, keepdims=True)
    e = jnp.exp(logits - top)
    return e / jnp.sum(e, axis=0, keepdims=True)


def rows(start, size):
    return pl.ds(pl.multiple_of(start, 16), size)


def lanes(start, size):
    return pl.ds(pl.multiple_of(start, 128), size)


def kernel(
    pview, rview, patches, rays, targets, slots_init, packed, camera,
    slots_out, colour_out, loss_out, gin_out, gro_out,
    cy0, cy1, cy2, cy3, f0, f1, f2, f3, sg0, sg1, sg2, sg3, camsg, camcy, camf,
    px, rin, rx, ro, state, tsend, trecv, tysend, tyrecv, tzsend, tzrecv,
    psend, precv, ssend, srecv, dcol8, small, smrecv_cx, smrecv_y, smrecv_z, smy, smz,
    jt, gown, gcs, gcr, gxs, gxr, gzs, gzr, gys, gyr, gfs, gfr,
    cy_s, cy_r, z_s, z_r, x_s, x_r, c_s, c_r, it_s, it_r, gr_s, gr_r,
):
    z, y, c, x = (lax.axis_index(a) for a in ("z", "y", "c", "x"))
    cyb, full, stage = (cy0, cy1, cy2, cy3), (f0, f1, f2, f3), (sg0, sg1, sg2, sg3)
    width = patches.shape[1]
    scale = width ** (-0.5)
    pending = []

    def send(src, dst, ssem, rsem, **where):
        cp = pltpu.make_async_remote_copy(
            src_ref=src, dst_ref=dst, send_sem=ssem, recv_sem=rsem,
            device_id=where, device_id_type=pl.DeviceIdType.MESH,
        )
        cp.start()
        pending.append(cp)
        return cp

    def yc_peers():
        return [(dy, dc) for dy in range(NY) for dc in range(NC) if dy or dc]

    def cx_peers():
        return [(dc, dx) for dc in range(NC) for dx in range(NX) if dc or dx]

    def flip(dc):
        return 1 - c if dc else c

    barrier = pltpu.get_barrier_semaphore()
    met = 0
    for dy, dc in yc_peers():
        pl.semaphore_signal(barrier, inc=1, device_id={"y": lax.rem(y + dy, NY), "c": flip(dc)}, device_id_type=pl.DeviceIdType.MESH)
        met += 1
    for dc, dx in cx_peers():
        if dx:
            pl.semaphore_signal(barrier, inc=1, device_id={"x": lax.rem(x + dx, NX), "c": flip(dc)}, device_id_type=pl.DeviceIdType.MESH)
            met += 1
    for dz in range(1, NZ):
        pl.semaphore_signal(barrier, inc=1, device_id={"z": lax.rem(z + dz, NZ)}, device_id_type=pl.DeviceIdType.MESH)
        met += 1
    pl.semaphore_wait(barrier, met)

    me_yc = y * 2 + c
    quarter = x * (1 - c) + y * c

    def along(d):
        return dict(x=lax.rem(x + d * (1 - c), NX), y=lax.rem(y + d * c, NY))

    def across(d):
        return dict(x=lax.rem(x + d * c, NX), y=lax.rem(y + d * (1 - c), NY))

    def yc_copies(src, buf, slot, w, part):
        out = []
        for k, (dy, dc) in enumerate(yc_peers()):
            yy, cc = lax.rem(y + dy, NY), flip(dc)
            cp = pltpu.make_async_remote_copy(
                src_ref=src.at[:, lanes(part(yy, cc) * w, w)], dst_ref=buf.at[rows(me_yc * 16, 16)],
                send_sem=cy_s.at[slot, k], recv_sem=cy_r.at[slot, k],
                device_id={"y": yy, "c": cc}, device_id_type=pl.DeviceIdType.MESH,
            )
            out.append((cp, dy, cc))
        return out

    def start_bundle(b):
        w = LEN[b] // NX
        stage[b][...] = packed[:, OFF[b] : OFF[b] + LEN[b]]
        cyb[b][rows(me_yc * 16, 16), :] = stage[b][:, lanes(quarter * w, w)]
        cps = yc_copies(stage[b], cyb[b], b, w, lambda yy, cc: x * (1 - cc) + yy * cc)
        for cp, dy, cc in cps:
            @pl.when(y // 2 == cc)
            def _():
                cp.start()

        return cps

    def finish_bundle(cps):
        for cp, dy, cc in cps:
            @pl.when(lax.rem(y - dy + NY, NY) // 2 == c)
            def _():
                cp.wait_recv()

            @pl.when(y // 2 == cc)
            def _():
                cp.wait_send()

    def compact(shards, real, first, count):
        n = shards.shape[0]
        r = lax.broadcasted_iota(jnp.int32, (count, n), 0) + first
        k = lax.broadcasted_iota(jnp.int32, (count, n), 1)
        lane = k % 16
        mask = (lane < real) & (r == (k // 16) * real + lane)
        return dot(onehot(mask), shards).astype(BF)

    def piece(b, zz):
        w = LEN[b] // NX
        return full[b].at[rows(zz * 96 + c * 48, 48), lanes(quarter * w, w)]

    def start_z(b, arrived):
        finish_bundle(arrived)
        w = LEN[b] // NX
        full[b][rows(z * 96 + c * 48, 48), lanes(quarter * w, w)] = compact(cyb[b][rows(c * 64, 64), :], 12, 0, 48)
        return [
            send(piece(b, z), piece(b, z), z_s.at[b, d], z_r.at[b, d], z=lax.rem(z + d, NZ))
            for d in range(1, NZ)
        ]

    def forward_x(b, ref, d):
        return [send(ref, ref, x_s.at[b, k, d], x_r.at[b, k, d], **along(k)) for k in range(1, NX)]

    def start_x(b, arriving):
        out = [forward_x(b, piece(b, z), 0)]
        for d in range(1, NZ):
            arriving[d - 1].wait()
            out.append(forward_x(b, piece(b, lax.rem(z - d + NZ, NZ)), d))
        return out

    def swap_core(b, arriving):
        cps = []
        for d in range(NZ):
            for cp in arriving[d]:
                cp.wait()
            ref = full[b].at[rows(lax.rem(z - d + NZ, NZ) * 96 + c * 48, 48)]
            cps.append(send(ref, ref, c_s.at[b, d], c_r.at[b, d], c=1 - c))
        return cps

    def done(cps):
        for cp in cps:
            cp.wait()

    half = width // 2
    cy_b0 = start_bundle(0)
    camsg[...] = camera[...]
    camcy[rows(me_yc * 16, 16), :] = camsg[:, lanes(c * half, half)]
    cy_cam = yc_copies(camsg, camcy, 4, half, lambda yy, cc: cc)
    for cp, _, _ in cy_cam:
        cp.start()
    n0 = normalize(slots_init[...]).astype(BF)
    z_b0 = start_z(0, cy_b0)
    for cp, _, _ in cy_cam:
        cp.wait()
    camf[rows(z * 64 + quarter * 16, 16), lanes(c * half, half)] = compact(camcy[...], 8, quarter * 16, 16)

    def cam_piece(zz):
        return camf.at[rows(zz * 64 + quarter * 16, 16), lanes(c * half, half)]

    z_cam = [
        send(cam_piece(z), cam_piece(z), z_s.at[4, d], z_r.at[4, d], z=lax.rem(z + d, NZ))
        for d in range(1, NZ)
    ]
    cy_b1 = start_bundle(1)
    cy_b2 = start_bundle(2)
    x_cam = forward_x(4, cam_piece(z), 0)
    for d in range(1, NZ):
        z_cam[d - 1].wait()
        x_cam += forward_x(4, cam_piece(lax.rem(z - d + NZ, NZ)), d)
    x_b0 = start_x(0, z_b0)
    z_b1 = start_z(1, cy_b1)
    z_b2 = start_z(2, cy_b2)
    done(x_cam)
    cam_half = camf.at[:, lanes(c * half, half)]
    done([send(cam_half, cam_half, c_s.at[4, 0], c_r.at[4, 0], c=1 - c)])

    def lookup(view):
        v = lax.broadcasted_iota(jnp.int32, (camf.shape[0], view.shape[1]), 0)
        return dot(onehot(v == view[...]), camf[...], 0, 0)

    px[...] = normalize(patches[...].astype(F32) + lookup(pview)).astype(BF)
    rin[...] = rays[...].astype(F32) + lookup(rview)
    rx[...] = rin[...].astype(BF)
    done(swap_core(0, x_b0))

    def slot_projection(normed):
        query = (dot(normed, f0[:, 0:width]) * scale).astype(BF)
        return dot(query, f0[:, width : 2 * width], 1, 1).astype(BF)

    group = c * NX + x
    mine = pl.ds(pl.multiple_of(group * 8, 8), 8)
    state[...] = slots_init[mine, :]
    proj = slot_projection(n0)
    x_b1 = x_b2 = x_b3 = cy_b3 = z_b3 = c_b3 = None

    def group_rows(buf, t):
        return jnp.concatenate([buf[t, g].astype(F32) for g in range(8)], axis=0)

    def share(t, value):
        psend[t] = value
        precv[t, group] = value
        return [
            send(psend.at[t], precv.at[t, group], it_s.at[t, 24 + k], it_r.at[t, 24 + k],
                 c=flip(dc), x=lax.rem(x + dx, NX))
            for k, (dc, dx) in enumerate(cx_peers())
        ]

    for t in range(ITERS):
        attn = softmax0(dot(proj, px[...], 1, 1)) + ATTN_FLOOR
        total = dot(attn.astype(BF), px[...])
        denom = jnp.sum(attn, axis=1, keepdims=True)
        for g in range(8):
            tsend[t, g, :, 0:width] = total[8 * g : 8 * g + 8].astype(BF)
            tsend[t, g, :, width : width + 128] = jnp.broadcast_to(denom[8 * g : 8 * g + 8], (8, 128)).astype(BF)
        cps = []
        for k, (dc, dx) in enumerate(cx_peers()):
            cc, xx = flip(dc), lax.rem(x + dx, NX)
            cps.append(send(tsend.at[t, cc * NX + xx], trecv.at[t, k], it_s.at[t, k], it_r.at[t, k], c=cc, x=xx))
        if t == 0:
            x_b1 = start_x(1, z_b1)
            x_b2 = start_x(2, z_b2)
            cy_b3 = start_bundle(3)
        if t == 1:
            x_b3 = start_x(3, z_b3)
        if t == 2:
            c_b3 = swap_core(3, x_b3)
        acc = tsend[t, group].astype(F32)
        for k, cp in enumerate(cps):
            cp.wait()
            acc += trecv[t, k].astype(F32)
        tysend[t] = acc.astype(BF)
        cps = [
            send(tysend.at[t], tyrecv.at[t, d], it_s.at[t, 8 + d], it_r.at[t, 8 + d], y=lax.rem(y + d, NY))
            for d in range(1, NY)
        ]
        for cp in cps:
            cp.wait()
        acc = ordered(tyrecv, tysend, t, y, NY)
        tzsend[t] = acc.astype(BF)
        cps = [
            send(tzsend.at[t], tzrecv.at[t, d], it_s.at[t, 12 + d], it_r.at[t, 12 + d], z=lax.rem(z + d, NZ))
            for d in range(1, NZ)
        ]
        if t == 0:
            c_b1 = swap_core(1, x_b1)
            c_b2 = swap_core(2, x_b2)
            z_b3 = start_z(3, cy_b3)
        for cp in cps:
            cp.wait()
        acc = ordered(tzrecv, tzsend, t, z, NZ)
        if t == 0:
            done(c_b1)
            done(c_b2)
        mean_x = (acc[:, 0:width] / acc[:, width : width + 1]).astype(BF)
        update = dot(mean_x, f1[:, 0:width]).astype(BF)
        slots = state[...]
        a = dot(update, f2[:, 0 : 3 * width])
        b = dot(slots.astype(BF), f2[:, 3 * width : 6 * width])
        reset = jax.nn.sigmoid(a[:, 0:width] + b[:, 0:width])
        blend = jax.nn.sigmoid(a[:, width : 2 * width] + b[:, width : 2 * width])
        cand = jnp.tanh(a[:, 2 * width :] + reset * b[:, 2 * width :])
        slots = (1.0 - blend) * cand + blend * slots
        state[...] = slots
        if t + 1 < ITERS:
            cps = share(t, slot_projection(normalize(slots).astype(BF)))
            done(cps)
            proj = group_rows(precv, t).astype(BF)

    t = ITERS - 1
    ssend[...] = slots
    srecv[mine, :] = slots
    s_cps = [
        send(ssend, srecv.at[mine], gr_s.at[0, k], gr_r.at[0, k], c=flip(dc), x=lax.rem(x + dx, NX))
        for k, (dc, dx) in enumerate(cx_peers())
    ]
    done(c_b3)
    slot_keys = dot(slots.astype(BF), f1[:, width : 2 * width]).astype(BF)
    r_cps = share(t, (dot(slot_keys, f3[:, 0:width], 1, 1) * scale).astype(BF))
    r = lax.broadcasted_iota(jnp.int32, (width, 1), 0)
    hid = 2 * r - r % 12
    unit = lax.broadcasted_iota(jnp.int32, (width, 2 * width), 1)
    ro[...] = (
        dot(f3[:, 3 * width : 3 * width + 128], onehot(unit == hid), 0, 0)
        + dot(f3[:, 3 * width + 128 : 3 * width + 256], onehot(unit == hid + 12), 0, 0)
    )[0:8].astype(BF)
    done(s_cps)
    done(r_cps)
    slots_all = srecv[...]
    slots_out[...] = slots_all
    low = slots_all.astype(BF)
    mix = softmax0(dot(group_rows(precv, t).astype(BF), rx[...], 1, 1)).astype(BF)
    joined = (dot(mix, low, 0, 0) + rin[...]).astype(BF)
    pre = dot(joined, f3[:, width : 3 * width])
    sig = jax.nn.sigmoid(pre)
    hidden = (pre * sig).astype(BF)
    colour = dot(ro[...], hidden, 1, 1)[0:3]
    colour_out[...] = colour
    error = colour - targets[...]
    rays_total = rin.shape[0] * NZ * NY * NC * NX
    dcol8[...] = jnp.zeros_like(dcol8)
    dcol8[0:3, :] = error * (2.0 / jnp.sqrt(jnp.float32(3.0 * rays_total)))
    dcol = dcol8[...].astype(BF)
    dpre = (dot(dcol, ro[...], 0, 0) * (sig + pre * sig * (1.0 - sig))).astype(BF)
    gro = dot(dcol, hidden)
    squared = jnp.sum(jnp.sum(error * error, axis=1, keepdims=True), axis=0, keepdims=True)

    turned = jnp.transpose(joined.astype(F32)).astype(BF)
    for zz in range(NZ):
        for h in range(NC):
            jt[384 * h + 48 * zz : 384 * h + 48 * zz + 48, :] = turned[96 * zz + 48 * h : 96 * zz + 48 * h + 48]
    gcs[...] = dot(jt[rows(384 * (1 - c), 384), :], dpre).astype(BF)
    g_c = send(gcs, gcr, gr_s.at[1, 0], gr_r.at[1, 0], c=1 - c)
    small[...] = jnp.zeros_like(small)
    small[0:3, :] = gro[0:3, 0:width]
    small[3:6, :] = gro[0:3, width:]
    small[6:7, :] = jnp.broadcast_to(squared, (1, width))
    sm_cps = [
        send(small, smrecv_cx.at[group], gr_s.at[2, k], gr_r.at[2, k], c=flip(dc), x=lax.rem(x + dx, NX))
        for k, (dc, dx) in enumerate(cx_peers())
    ]
    smrecv_cx[group] = small[...]
    gown[...] = dot(jt[rows(384 * c, 384), :], dpre)
    g_c.wait()
    gown[...] += gcr[...].astype(F32)
    gxs[...] = gown[...].astype(BF)
    qw = 2 * width // NX
    gx = [
        send(gxs.at[:, lanes(lax.rem(quarter + d, NX) * qw, qw)], gxr.at[d], gr_s.at[3, d], gr_r.at[3, d], **along(d))
        for d in range(1, NX)
    ]
    done(sm_cps)
    acc_s = sum_of(smrecv_cx, 8)
    smy[...] = acc_s
    smrecv_y[y] = acc_s
    sm_cps = [
        send(smy, smrecv_y.at[y], gr_s.at[4, d], gr_r.at[4, d], y=lax.rem(y + d, NY)) for d in range(1, NY)
    ]
    done(sm_cps)
    acc_s = sum_of(smrecv_y, NY)
    smz[...] = acc_s
    smrecv_z[z] = acc_s
    sm_cps = [
        send(smz, smrecv_z.at[z], gr_s.at[5, d], gr_r.at[5, d], z=lax.rem(z + d, NZ)) for d in range(1, NZ)
    ]
    acc_g = gown[:, lanes(quarter * qw, qw)]
    for d, cp in enumerate(gx):
        cp.wait()
        acc_g += gxr[d + 1].astype(F32)
    gzs[...] = acc_g.astype(BF)
    gz = [
        send(gzs.at[rows(lax.rem(z + d, NZ) * 48, 48)], gzr.at[d], gr_s.at[6, d], gr_r.at[6, d], z=lax.rem(z + d, NZ))
        for d in range(1, NZ)
    ]
    done(sm_cps)
    acc_s = sum_of(smrecv_z, NZ)
    gro_out[:, 0:width] = acc_s[0:3]
    gro_out[:, width:] = acc_s[3:6]
    loss_out[...] = acc_s[6:7, 0:1] / (3.0 * rays_total)
    acc_g = gzs[rows(z * 48, 48), :].astype(F32)
    for d, cp in enumerate(gz):
        cp.wait()
        acc_g += gzr[d + 1].astype(F32)
    gys[0] = acc_g.astype(BF)
    for cp in [send(gys.at[0], gyr.at[0, d], gr_s.at[7, d], gr_r.at[7, d], **across(d)) for d in range(1, NY)]:
        cp.wait()
    place = x * c + y * (1 - c)
    gfs[...] = ordered(gyr, gys, 0, place, NY)

    def final(k, row, slot, **where):
        return pltpu.make_async_remote_copy(
            src_ref=gfs.at[pl.ds(pl.multiple_of(row * 24, 8), 24)], dst_ref=gfr.at[slot],
            send_sem=gr_s.at[8, k], recv_sem=gr_r.at[8, slot],
            device_id=where, device_id_type=pl.DeviceIdType.MESH,
        )

    low_half = y // 2 == 0
    keeps = y // 2 == c
    own_row = lax.rem(y, 2)

    @pl.when(keeps)
    def _():
        gfr[quarter] = gfs[pl.ds(pl.multiple_of(own_row * 24, 8), 24), :]

    def to_x(act):
        for k, (dc, dx) in enumerate(cx_peers()):
            act(final(k, own_row, quarter, c=flip(dc), x=lax.rem(x + dx, NX)))

    def to_y(act):
        for k in range(4):
            yy, cc = 2 + k // 2, k % 2

            @pl.when(jnp.logical_not((y == yy) & (c == cc)))
            def _():
                act(final(k, k // 2, quarter, y=yy, c=cc))

    @pl.when((c == 0) & low_half)
    def _():
        to_x(lambda cp: cp.start())

    @pl.when(c == 1)
    def _():
        to_y(lambda cp: cp.start())

    for slot in range(NX):
        @pl.when(jnp.logical_not(keeps & (quarter == slot)))
        def _():
            final(0, 0, slot, c=1 - c).wait_recv()

        blk = gfr[slot]
        gin_out[:, qw * slot : qw * slot + qw] = jnp.where(c == 0, blk[0:12], blk[12:24])

    @pl.when((c == 0) & low_half)
    def _():
        to_x(lambda cp: cp.wait_send())

    @pl.when(c == 1)
    def _():
        to_y(lambda cp: cp.wait_send())


def sum_of(buf, n):
    acc = buf[0]
    for j in range(1, n):
        acc += buf[j]
    return acc


def ordered(recv, own, t, me, n):
    acc = None
    for j in range(n):
        d = lax.rem(me - j + n, n)
        val = jnp.where(d == 0, own[t].astype(F32), recv[t, d].astype(F32))
        acc = val if acc is None else acc + val
    return acc


def on_device(
    patches, patch_view, rays, ray_view, targets, camera, slots_init, key_weight, value_weight,
    query_weight, gru_input, gru_hidden, mix_query, mix_key, render_in, render_out,
):
    n, width = patches.shape
    units = jnp.pad(render_out.T, ((0, 0), (0, 125)))
    pair = jnp.concatenate([units[0:12], units[12:24]], axis=1)
    packed = jnp.concatenate(
        [query_weight, key_weight, value_weight, mix_key, gru_input, gru_hidden, mix_query, render_in, pair], axis=1
    )
    packed = jnp.pad(packed, ((0, 4), (0, 0)))
    cam = jnp.pad(camera, ((0, 8), (0, 0)))
    V, S = pltpu.VMEM, pltpu.SemaphoreType.DMA
    vm = pl.BlockSpec(memory_space=pltpu.VMEM)
    scratch = (
        [V((128, L // NX), BF) for L in LEN]
        + [V((width, L), BF) for L in LEN]
        + [V((16, L), BF) for L in LEN]
        + [
            V((16, width), BF), V((128, width // 2), BF), V((512, width), BF),
            V((n, width), BF), V((n, width), F32), V((n, width), BF), V((8, 2 * width), BF), V((8, width), F32),
            V((3, 8, 8, width + 128), BF), V((3, 8, 8, width + 128), BF),
            V((3, 8, width + 128), BF), V((3, NY, 8, width + 128), BF),
            V((3, 8, width + 128), BF), V((3, NZ, 8, width + 128), BF),
            V((3, 8, width), BF), V((3, 8, 8, width), BF), V((8, width), F32), V((64, width), F32),
            V((8, n), F32), V((8, width), F32), V((8, 8, width), F32), V((NY, 8, width), F32), V((NZ, 8, width), F32),
            V((8, width), F32), V((8, width), F32),
            V((width, n), BF), V((384, 2 * width), F32), V((384, 2 * width), BF), V((384, 2 * width), BF),
            V((384, 2 * width), BF), V((NX, 384, width // 2), BF), V((384, width // 2), BF), V((NZ, 48, width // 2), BF),
            V((1, 48, width // 2), BF), V((1, NY, 48, width // 2), BF), V((48, width // 2), F32), V((NX, 24, width // 2), F32),
            S((5, 7)), S((5, 7)), S((5, 8)), S((5, 8)), S((5, 4, 8)), S((5, 4, 8)), S((5, 8)), S((5, 8)),
            S((3, 32)), S((3, 32)), S((9, 8)), S((9, 8)),
        ]
    )
    out = pl.pallas_call(
        kernel,
        out_shape=[
            jax.ShapeDtypeStruct((64, width), F32),
            jax.ShapeDtypeStruct((3, n), F32),
            jax.ShapeDtypeStruct((1, 1), F32),
            jax.ShapeDtypeStruct((12, 2 * width), F32),
            jax.ShapeDtypeStruct((3, 2 * width), F32),
        ],
        in_specs=[vm] * 8,
        out_specs=[vm] * 5,
        scratch_shapes=scratch,
        compiler_params=pltpu.CompilerParams(collective_id=0, has_side_effects=True, vmem_limit_bytes=60 << 20),
    )(patch_view[None], ray_view[None], patches, rays, targets, slots_init, packed, cam)
    slots, colour, loss, gin, gro = out
    return slots, colour, loss[0, 0], gin, gro


def solution(mesh):
    torus = Mesh(mesh.devices.reshape(NZ, NY, NC, NX), ("z", "y", "c", "x"))
    tok, every = ("z", "y", "c"), ("z", "y", "c", "x")
    w = P(tok, None)
    return jax.shard_map(
        on_device,
        mesh=torus,
        in_specs=(
            P(every, None), P(every), P(every, None), P(every), P(None, every), w, P(),
            w, w, w, w, w, w, w, w, P(None, tok),
        ),
        out_specs=(P(), P(None, every), P(), w, P()),
        check_vma=False,
    )
```

```python
import functools

import jax
import jax.numpy as jnp
from jax import lax
from jax.experimental import pallas as pl
from jax.experimental.pallas import tpu as pltpu
from jax.sharding import Mesh
from jax.sharding import PartitionSpec as P

ITERS = 3
EPSILON = 1e-05
ATTN_FLOOR = 1e-08
NZ, NY, NC, NX = 8, 4, 2, 4
BF = jnp.bfloat16
F32 = jnp.float32

LEN = (1536, 1536, 4608, 2560)
NB = 4


def dot(a, b, ca=1, cb=0):
    return lax.dot_general(a, b, (((ca,), (cb,)), ((), ())), preferred_element_type=F32)


def normalize(values):
    mean = jnp.mean(values, axis=-1, keepdims=True)
    centred = values - mean
    spread = jnp.mean(centred * centred, axis=-1, keepdims=True)
    return centred * lax.rsqrt(spread + EPSILON)


def onehot(mask):
    return mask.astype(F32).astype(BF)


def softmax0(logits):
    top = jnp.max(logits, axis=0, keepdims=True)
    e = jnp.exp(logits - top)
    return e / jnp.sum(e, axis=0, keepdims=True)


def rows(start, size):
    return pl.ds(pl.multiple_of(start, 16), size)


def lanes(start, size):
    return pl.ds(pl.multiple_of(start, 128), size)


def kernel(
    pview, rview, patches, rays, targets, slots_init, camera,
    wq, wk, wv, mk, gi, gh, mq, rin_w, rout,
    slots_out, colour_out, loss_out, gin_out, gro_out,
    cy0, cy1, cy2, cy3, f0, f1, f2, f3, sg0, sg1, sg2, sg3, rp, camsg, camcy, camf,
    px, rin, rx, ro, state, tsend, trecv, tysend, tyrecv, tzsend, tzrecv,
    psend, precv, ssend, srecv, dcol8, small, smrecv_cx, smrecv_y, smrecv_z, smy, smz,
    jt, gown, gcs, gcr, gxs, gxr, gzs, gzr, gys, gyr, gfs, gfr,
    cy_s, cy_r, z_s, z_r, x_s, x_r, c_s, c_r, it_s, it_r, gr_s, gr_r,
):
    z, y, c, x = (lax.axis_index(a) for a in ("z", "y", "c", "x"))
    cyb, full, stage = (cy0, cy1, cy2, cy3), (f0, f1, f2, f3), (sg0, sg1, sg2, sg3)
    width = patches.shape[1]
    scale = width ** (-0.5)
    pending = []

    def send(src, dst, ssem, rsem, **where):
        cp = pltpu.make_async_remote_copy(
            src_ref=src, dst_ref=dst, send_sem=ssem, recv_sem=rsem,
            device_id=where, device_id_type=pl.DeviceIdType.MESH,
        )
        cp.start()
        pending.append(cp)
        return cp

    def yc_peers():
        return [(dy, dc) for dy in range(NY) for dc in range(NC) if dy or dc]

    def cx_peers():
        return [(dc, dx) for dc in range(NC) for dx in range(NX) if dc or dx]

    def flip(dc):
        return 1 - c if dc else c

    barrier = pltpu.get_barrier_semaphore()
    met = 0
    for dy, dc in yc_peers():
        pl.semaphore_signal(barrier, inc=1, device_id={"y": lax.rem(y + dy, NY), "c": flip(dc)}, device_id_type=pl.DeviceIdType.MESH)
        met += 1
    for dc, dx in cx_peers():
        if dx:
            pl.semaphore_signal(barrier, inc=1, device_id={"x": lax.rem(x + dx, NX), "c": flip(dc)}, device_id_type=pl.DeviceIdType.MESH)
            met += 1
    for dz in range(1, NZ):
        pl.semaphore_signal(barrier, inc=1, device_id={"z": lax.rem(z + dz, NZ)}, device_id_type=pl.DeviceIdType.MESH)
        met += 1
    pl.semaphore_wait(barrier, met)

    me_yc = y * 2 + c
    quarter = x * (1 - c) + y * c

    def along(d):
        return dict(x=lax.rem(x + d * (1 - c), NX), y=lax.rem(y + d * c, NY))

    def across(d):
        return dict(x=lax.rem(x + d * c, NX), y=lax.rem(y + d * (1 - c), NY))

    def yc_copies(src, buf, slot, w, part):
        out = []
        for k, (dy, dc) in enumerate(yc_peers()):
            yy, cc = lax.rem(y + dy, NY), flip(dc)
            cp = pltpu.make_async_remote_copy(
                src_ref=src.at[:, lanes(part(yy, cc) * w, w)], dst_ref=buf.at[rows(me_yc * 16, 16)],
                send_sem=cy_s.at[slot, k], recv_sem=cy_r.at[slot, k],
                device_id={"y": yy, "c": cc}, device_id_type=pl.DeviceIdType.MESH,
            )
            out.append((cp, dy, cc))
        return out

    def pack(b, parts):
        stage[b][...] = jnp.zeros_like(stage[b])
        at = 0
        for part in parts:
            stage[b][0:12, at : at + part.shape[1]] = part[...]
            at += part.shape[1]

    def pack_colour(at):
        rp[...] = jnp.zeros_like(rp)
        rp[0:3, :] = rout[...].astype(F32)
        unit = lax.broadcasted_iota(jnp.int32, (16, 24), 1)
        row = lax.broadcasted_iota(jnp.int32, (16, 24), 0)
        for j in range(2):
            mask = (unit == row + 12 * j) & (row < 12)
            stage[3][:, at + 128 * j : at + 128 * j + 128] = dot(onehot(mask), rp[...].astype(BF), 1, 1).astype(BF)

    def start_bundle(b):
        w = LEN[b] // NX
        cyb[b][rows(me_yc * 16, 16), :] = stage[b][:, lanes(quarter * w, w)]
        cps = yc_copies(stage[b], cyb[b], b, w, lambda yy, cc: x * (1 - cc) + yy * cc)
        for cp, dy, cc in cps:
            @pl.when(y // 2 == cc)
            def _():
                cp.start()

        return cps

    def finish_bundle(cps):
        for cp, dy, cc in cps:
            @pl.when(lax.rem(y - dy + NY, NY) // 2 == c)
            def _():
                cp.wait_recv()

            @pl.when(y // 2 == cc)
            def _():
                cp.wait_send()

    def compact(shards, real, first, count):
        n = shards.shape[0]
        r = lax.broadcasted_iota(jnp.int32, (count, n), 0) + first
        k = lax.broadcasted_iota(jnp.int32, (count, n), 1)
        lane = k % 16
        mask = (lane < real) & (r == (k // 16) * real + lane)
        return dot(onehot(mask), shards).astype(BF)

    def piece(b, zz):
        w = LEN[b] // NX
        return full[b].at[rows(zz * 96 + c * 48, 48), lanes(quarter * w, w)]

    def start_z(b, arrived, ring=True):
        finish_bundle(arrived)
        w = LEN[b] // NX
        full[b][rows(z * 96 + c * 48, 48), lanes(quarter * w, w)] = compact(cyb[b][rows(c * 64, 64), :], 12, 0, 48)
        if not ring:
            return [
                send(piece(b, z), piece(b, z), z_s.at[b, d], z_r.at[b, d], z=lax.rem(z + d, NZ))
                for d in range(1, NZ)
            ]
        return [pass_on(b, z, 1), pass_on(b, z, NZ - 1)]

    def pass_on(b, zz, d):
        to = lax.rem(z + (1 if d <= NZ // 2 else NZ - 1), NZ)
        return send(piece(b, zz), piece(b, zz), z_s.at[b, d], z_r.at[b, d], z=to)

    def forward_x(b, ref, d):
        return [send(ref, ref, x_s.at[b, k, d], x_r.at[b, k, d], **along(k)) for k in range(1, NX)]

    def start_x(b, arriving):
        out = [(0, forward_x(b, piece(b, z), 0))]
        for d in range(1, NZ):
            arriving[d - 1].wait()
            out.append((d, forward_x(b, piece(b, lax.rem(z - d + NZ, NZ)), d)))
        return out, []

    def ring_x(bundles):
        out = {b: [(0, forward_x(b, piece(b, z), 0))] for b, _ in bundles}
        sent = {b: list(first) for b, first in bundles}
        for k in range(1, NZ // 2 + 1):
            for d in (k, NZ - k) if k < NZ // 2 else (k,):
                for b, _ in bundles:
                    zz = lax.rem(z - d + NZ, NZ)
                    pltpu.make_async_remote_copy(
                        src_ref=piece(b, zz), dst_ref=piece(b, zz), send_sem=z_s.at[b, d], recv_sem=z_r.at[b, d],
                        device_id={"z": zz}, device_id_type=pl.DeviceIdType.MESH,
                    ).wait_recv()
                    if d < NZ // 2:
                        sent[b].append(pass_on(b, zz, d + 1))
                    if d > NZ // 2 + 1:
                        sent[b].append(pass_on(b, zz, d - 1))
                    out[b].append((d, forward_x(b, piece(b, zz), d)))
        return {b: (out[b], sent[b]) for b, _ in bundles}

    def swap_core(b, gathered):
        arriving, sent = gathered
        for cp in sent:
            cp.wait_send()
        cps = []
        for d, group_cps in arriving:
            for cp in group_cps:
                cp.wait()
            ref = full[b].at[rows(lax.rem(z - d + NZ, NZ) * 96 + c * 48, 48)]
            cps.append(send(ref, ref, c_s.at[b, d], c_r.at[b, d], c=1 - c))
        return cps

    def done(cps):
        for cp in cps:
            cp.wait()

    half = width // 2
    pack(0, (wq, wk))
    cy_b0 = start_bundle(0)
    camsg[...] = jnp.zeros_like(camsg)
    camsg[0:8, :] = camera[...]
    camcy[rows(me_yc * 16, 16), :] = camsg[:, lanes(c * half, half)]
    cy_cam = yc_copies(camsg, camcy, 4, half, lambda yy, cc: cc)
    for cp, _, _ in cy_cam:
        cp.start()
    n0 = normalize(slots_init[...]).astype(BF)
    z_b0 = start_z(0, cy_b0)
    for cp, _, _ in cy_cam:
        cp.wait()
    camf[rows(z * 64 + quarter * 16, 16), lanes(c * half, half)] = compact(camcy[...], 8, quarter * 16, 16)

    def cam_piece(zz):
        return camf.at[rows(zz * 64 + quarter * 16, 16), lanes(c * half, half)]

    z_cam = [
        send(cam_piece(z), cam_piece(z), z_s.at[4, d], z_r.at[4, d], z=lax.rem(z + d, NZ))
        for d in range(1, NZ)
    ]
    pack(1, (wv, mk))
    cy_b1 = start_bundle(1)
    pack(2, (gi, gh))
    cy_b2 = start_bundle(2)
    x_b0 = ring_x([(0, z_b0)])[0]
    z_b1 = start_z(1, cy_b1)
    z_b2 = start_z(2, cy_b2)
    x_cam = forward_x(4, cam_piece(z), 0)
    for d in range(1, NZ):
        z_cam[d - 1].wait()
        x_cam += forward_x(4, cam_piece(lax.rem(z - d + NZ, NZ)), d)
    pack(3, (mq, rin_w))
    pack_colour(3 * width)
    cy_b3 = start_bundle(3)
    c_b0 = swap_core(0, x_b0)
    bulk = ring_x([(1, z_b1), (2, z_b2)])
    z_b3 = start_z(3, cy_b3, ring=False)
    done(x_cam)
    cam_half = camf.at[:, lanes(c * half, half)]
    done([send(cam_half, cam_half, c_s.at[4, 0], c_r.at[4, 0], c=1 - c)])

    def lookup(view):
        v = lax.broadcasted_iota(jnp.int32, (camf.shape[0], view.shape[1]), 0)
        return dot(onehot(v == view[...]), camf[...], 0, 0)

    px[...] = normalize(patches[...].astype(F32) + lookup(pview)).astype(BF)
    rin[...] = rays[...].astype(F32) + lookup(rview)
    rx[...] = rin[...].astype(BF)
    done(c_b0)

    def slot_projection(normed):
        query = (dot(normed, f0[:, 0:width]) * scale).astype(BF)
        return dot(query, f0[:, width : 2 * width], 1, 1).astype(BF)

    group = c * NX + x
    mine = pl.ds(pl.multiple_of(group * 8, 8), 8)
    state[...] = slots_init[mine, :]
    proj = slot_projection(n0)
    x_b3 = c_b3 = None

    def group_rows(buf, t):
        return jnp.concatenate([buf[t, g].astype(F32) for g in range(8)], axis=0)

    def share(t, value):
        psend[t] = value
        precv[t, group] = value
        return [
            send(psend.at[t], precv.at[t, group], it_s.at[t, 24 + k], it_r.at[t, 24 + k],
                 c=flip(dc), x=lax.rem(x + dx, NX))
            for k, (dc, dx) in enumerate(cx_peers())
        ]

    for t in range(ITERS):
        attn = softmax0(dot(proj, px[...], 1, 1)) + ATTN_FLOOR
        total = dot(attn.astype(BF), px[...])
        denom = jnp.sum(attn, axis=1, keepdims=True)
        for g in range(8):
            tsend[t, g, :, 0:width] = total[8 * g : 8 * g + 8].astype(BF)
            tsend[t, g, :, width : width + 128] = jnp.broadcast_to(denom[8 * g : 8 * g + 8], (8, 128)).astype(BF)
        cps = []
        for k, (dc, dx) in enumerate(cx_peers()):
            cc, xx = flip(dc), lax.rem(x + dx, NX)
            cps.append(send(tsend.at[t, cc * NX + xx], trecv.at[t, k], it_s.at[t, k], it_r.at[t, k], c=cc, x=xx))
        acc = tsend[t, group].astype(F32)
        for k, cp in enumerate(cps):
            cp.wait()
            acc += trecv[t, k].astype(F32)
        tysend[t] = acc.astype(BF)
        cps = [
            send(tysend.at[t], tyrecv.at[t, d], it_s.at[t, 8 + d], it_r.at[t, 8 + d], y=lax.rem(y + d, NY))
            for d in range(1, NY)
        ]
        for cp in cps:
            cp.wait()
        acc = ordered(tyrecv, tysend, t, y, NY)
        tzsend[t] = acc.astype(BF)
        cps = [
            send(tzsend.at[t], tzrecv.at[t, d], it_s.at[t, 12 + d], it_r.at[t, 12 + d], z=lax.rem(z + d, NZ))
            for d in range(1, NZ)
        ]
        if t == 0:
            c_b1 = swap_core(1, bulk[1])
            c_b2 = swap_core(2, bulk[2])
        if t == 1:
            c_b3 = swap_core(3, x_b3)
        for cp in cps:
            cp.wait()
        acc = ordered(tzrecv, tzsend, t, z, NZ)
        if t == 0:
            x_b3 = start_x(3, z_b3)
            done(c_b1)
            done(c_b2)
        mean_x = (acc[:, 0:width] / acc[:, width : width + 1]).astype(BF)
        update = dot(mean_x, f1[:, 0:width]).astype(BF)
        slots = state[...]
        a = dot(update, f2[:, 0 : 3 * width])
        b = dot(slots.astype(BF), f2[:, 3 * width : 6 * width])
        reset = jax.nn.sigmoid(a[:, 0:width] + b[:, 0:width])
        blend = jax.nn.sigmoid(a[:, width : 2 * width] + b[:, width : 2 * width])
        cand = jnp.tanh(a[:, 2 * width :] + reset * b[:, 2 * width :])
        slots = (1.0 - blend) * cand + blend * slots
        state[...] = slots
        if t + 1 < ITERS:
            cps = share(t, slot_projection(normalize(slots).astype(BF)))
            done(cps)
            proj = group_rows(precv, t).astype(BF)

    t = ITERS - 1
    ssend[...] = slots
    srecv[mine, :] = slots
    s_cps = [
        send(ssend, srecv.at[mine], gr_s.at[0, k], gr_r.at[0, k], c=flip(dc), x=lax.rem(x + dx, NX))
        for k, (dc, dx) in enumerate(cx_peers())
    ]
    done(c_b3)
    slot_keys = dot(slots.astype(BF), f1[:, width : 2 * width]).astype(BF)
    r_cps = share(t, (dot(slot_keys, f3[:, 0:width], 1, 1) * scale).astype(BF))
    r = lax.broadcasted_iota(jnp.int32, (width, 1), 0)
    hid = 2 * r - r % 12
    unit = lax.broadcasted_iota(jnp.int32, (width, 2 * width), 1)
    ro[...] = (
        dot(f3[:, 3 * width : 3 * width + 128], onehot(unit == hid), 0, 0)
        + dot(f3[:, 3 * width + 128 : 3 * width + 256], onehot(unit == hid + 12), 0, 0)
    )[0:8].astype(BF)
    done(s_cps)
    done(r_cps)
    slots_all = srecv[...]
    slots_out[...] = slots_all
    low = slots_all.astype(BF)
    mix = softmax0(dot(group_rows(precv, t).astype(BF), rx[...], 1, 1)).astype(BF)
    joined = (dot(mix, low, 0, 0) + rin[...]).astype(BF)
    pre = dot(joined, f3[:, width : 3 * width])
    sig = jax.nn.sigmoid(pre)
    hidden = (pre * sig).astype(BF)
    colour = dot(ro[...], hidden, 1, 1)[0:3]
    colour_out[...] = colour
    error = colour - targets[...]
    rays_total = rin.shape[0] * NZ * NY * NC * NX
    dcol8[...] = jnp.zeros_like(dcol8)
    dcol8[0:3, :] = error * (2.0 / jnp.sqrt(jnp.float32(3.0 * rays_total)))
    dcol = dcol8[...].astype(BF)
    dpre = (dot(dcol, ro[...], 0, 0) * (sig + pre * sig * (1.0 - sig))).astype(BF)
    gro = dot(dcol, hidden)
    squared = jnp.sum(jnp.sum(error * error, axis=1, keepdims=True), axis=0, keepdims=True)

    turned = jnp.transpose(joined.astype(F32)).astype(BF)
    for zz in range(NZ):
        for h in range(NC):
            jt[384 * h + 48 * zz : 384 * h + 48 * zz + 48, :] = turned[96 * zz + 48 * h : 96 * zz + 48 * h + 48]
    gcs[...] = dot(jt[rows(384 * (1 - c), 384), :], dpre).astype(BF)
    g_c = send(gcs, gcr, gr_s.at[1, 0], gr_r.at[1, 0], c=1 - c)
    small[...] = jnp.zeros_like(small)
    small[0:3, :] = gro[0:3, 0:width]
    small[3:6, :] = gro[0:3, width:]
    small[6:7, :] = jnp.broadcast_to(squared, (1, width))
    sm_cps = [
        send(small, smrecv_cx.at[group], gr_s.at[2, k], gr_r.at[2, k], c=flip(dc), x=lax.rem(x + dx, NX))
        for k, (dc, dx) in enumerate(cx_peers())
    ]
    smrecv_cx[group] = small[...]
    gown[...] = dot(jt[rows(384 * c, 384), :], dpre)
    g_c.wait()
    gown[...] += gcr[...].astype(F32)
    gxs[...] = gown[...].astype(BF)
    qw = 2 * width // NX
    gx = [
        send(gxs.at[:, lanes(lax.rem(quarter + d, NX) * qw, qw)], gxr.at[d], gr_s.at[3, d], gr_r.at[3, d], **along(d))
        for d in range(1, NX)
    ]
    done(sm_cps)
    acc_s = sum_of(smrecv_cx, 8)
    smy[...] = acc_s
    smrecv_y[y] = acc_s
    sm_cps = [
        send(smy, smrecv_y.at[y], gr_s.at[4, d], gr_r.at[4, d], y=lax.rem(y + d, NY)) for d in range(1, NY)
    ]
    done(sm_cps)
    acc_s = sum_of(smrecv_y, NY)
    smz[...] = acc_s
    smrecv_z[z] = acc_s
    sm_cps = [
        send(smz, smrecv_z.at[z], gr_s.at[5, d], gr_r.at[5, d], z=lax.rem(z + d, NZ)) for d in range(1, NZ)
    ]
    acc_g = gown[:, lanes(quarter * qw, qw)]
    for d, cp in enumerate(gx):
        cp.wait()
        acc_g += gxr[d + 1].astype(F32)
    gzs[...] = acc_g.astype(BF)
    gz = [
        send(gzs.at[rows(lax.rem(z + d, NZ) * 48, 48)], gzr.at[d], gr_s.at[6, d], gr_r.at[6, d], z=lax.rem(z + d, NZ))
        for d in range(1, NZ)
    ]
    done(sm_cps)
    acc_s = sum_of(smrecv_z, NZ)
    gro_out[:, 0:width] = acc_s[0:3]
    gro_out[:, width:] = acc_s[3:6]
    loss_out[...] = acc_s[6:7, 0:1] / (3.0 * rays_total)
    acc_g = gzs[rows(z * 48, 48), :].astype(F32)
    for d, cp in enumerate(gz):
        cp.wait()
        acc_g += gzr[d + 1].astype(F32)
    gys[0] = acc_g.astype(BF)
    for cp in [send(gys.at[0], gyr.at[0, d], gr_s.at[7, d], gr_r.at[7, d], **across(d)) for d in range(1, NY)]:
        cp.wait()
    place = x * c + y * (1 - c)
    gfs[...] = ordered(gyr, gys, 0, place, NY)

    def final(k, row, slot, **where):
        return pltpu.make_async_remote_copy(
            src_ref=gfs.at[pl.ds(pl.multiple_of(row * 24, 8), 24)], dst_ref=gfr.at[slot],
            send_sem=gr_s.at[8, k], recv_sem=gr_r.at[8, slot],
            device_id=where, device_id_type=pl.DeviceIdType.MESH,
        )

    low_half = y // 2 == 0
    keeps = y // 2 == c
    own_row = lax.rem(y, 2)

    @pl.when(keeps)
    def _():
        gfr[quarter] = gfs[pl.ds(pl.multiple_of(own_row * 24, 8), 24), :]

    def to_x(act):
        for k, (dc, dx) in enumerate(cx_peers()):
            act(final(k, own_row, quarter, c=flip(dc), x=lax.rem(x + dx, NX)))

    def to_y(act):
        for k in range(4):
            yy, cc = 2 + k // 2, k % 2

            @pl.when(jnp.logical_not((y == yy) & (c == cc)))
            def _():
                act(final(k, k // 2, quarter, y=yy, c=cc))

    @pl.when((c == 0) & low_half)
    def _():
        to_x(lambda cp: cp.start())

    @pl.when(c == 1)
    def _():
        to_y(lambda cp: cp.start())

    for slot in range(NX):
        @pl.when(jnp.logical_not(keeps & (quarter == slot)))
        def _():
            final(0, 0, slot, c=1 - c).wait_recv()

        blk = gfr[slot]
        gin_out[:, qw * slot : qw * slot + qw] = jnp.where(c == 0, blk[0:12], blk[12:24])

    @pl.when((c == 0) & low_half)
    def _():
        to_x(lambda cp: cp.wait_send())

    @pl.when(c == 1)
    def _():
        to_y(lambda cp: cp.wait_send())


def sum_of(buf, n):
    acc = buf[0]
    for j in range(1, n):
        acc += buf[j]
    return acc


def ordered(recv, own, t, me, n):
    acc = None
    for j in range(n):
        d = lax.rem(me - j + n, n)
        val = jnp.where(d == 0, own[t].astype(F32), recv[t, d].astype(F32))
        acc = val if acc is None else acc + val
    return acc


def on_device(
    patches, patch_view, rays, ray_view, targets, camera, slots_init, key_weight, value_weight,
    query_weight, gru_input, gru_hidden, mix_query, mix_key, render_in, render_out,
):
    n, width = patches.shape
    V, S = pltpu.VMEM, pltpu.SemaphoreType.DMA
    vm = pl.BlockSpec(memory_space=pltpu.VMEM)
    scratch = (
        [V((128, L // NX), BF) for L in LEN]
        + [V((width, L), BF) for L in LEN]
        + [V((16, L), BF) for L in LEN]
        + [
            V((128, 24), F32), V((16, width), BF), V((128, width // 2), BF), V((512, width), BF),
            V((n, width), BF), V((n, width), F32), V((n, width), BF), V((8, 2 * width), BF), V((8, width), F32),
            V((3, 8, 8, width + 128), BF), V((3, 8, 8, width + 128), BF),
            V((3, 8, width + 128), BF), V((3, NY, 8, width + 128), BF),
            V((3, 8, width + 128), BF), V((3, NZ, 8, width + 128), BF),
            V((3, 8, width), BF), V((3, 8, 8, width), BF), V((8, width), F32), V((64, width), F32),
            V((8, n), F32), V((8, width), F32), V((8, 8, width), F32), V((NY, 8, width), F32), V((NZ, 8, width), F32),
            V((8, width), F32), V((8, width), F32),
            V((width, n), BF), V((384, 2 * width), F32), V((384, 2 * width), BF), V((384, 2 * width), BF),
            V((384, 2 * width), BF), V((NX, 384, width // 2), BF), V((384, width // 2), BF), V((NZ, 48, width // 2), BF),
            V((1, 48, width // 2), BF), V((1, NY, 48, width // 2), BF), V((48, width // 2), F32), V((NX, 24, width // 2), F32),
            S((5, 7)), S((5, 7)), S((5, 8)), S((5, 8)), S((5, 4, 8)), S((5, 4, 8)), S((5, 8)), S((5, 8)),
            S((3, 32)), S((3, 32)), S((9, 8)), S((9, 8)),
        ]
    )
    out = pl.pallas_call(
        kernel,
        out_shape=[
            jax.ShapeDtypeStruct((64, width), F32),
            jax.ShapeDtypeStruct((3, n), F32),
            jax.ShapeDtypeStruct((1, 1), F32),
            jax.ShapeDtypeStruct((12, 2 * width), F32),
            jax.ShapeDtypeStruct((3, 2 * width), F32),
        ],
        in_specs=[vm] * 16,
        out_specs=[vm] * 5,
        scratch_shapes=scratch,
        compiler_params=pltpu.CompilerParams(collective_id=0, has_side_effects=True, vmem_limit_bytes=60 << 20),
    )(
        patch_view[None], ray_view[None], patches, rays, targets, slots_init, camera, query_weight, key_weight,
        value_weight, mix_key, gru_input, gru_hidden, mix_query, render_in, render_out,
    )
    slots, colour, loss, gin, gro = out
    return slots, colour, loss[0, 0], gin, gro


def solution(mesh):
    torus = Mesh(mesh.devices.reshape(NZ, NY, NC, NX), ("z", "y", "c", "x"))
    tok, every = ("z", "y", "c"), ("z", "y", "c", "x")
    w = P(tok, None)
    return jax.shard_map(
        on_device,
        mesh=torus,
        in_specs=(
            P(every, None), P(every), P(every, None), P(every), P(None, every), w, P(),
            w, w, w, w, w, w, w, w, P(None, tok),
        ),
        out_specs=(P(), P(None, every), P(), w, P()),
        check_vma=False,
    )
```

```python
import functools

import jax
import jax.numpy as jnp
from jax import lax
from jax.experimental import pallas as pl
from jax.experimental.pallas import tpu as pltpu
from jax.sharding import Mesh
from jax.sharding import PartitionSpec as P

ITERS = 3
EPSILON = 1e-05
ATTN_FLOOR = 1e-08
NZ, NY, NC, NX = 8, 4, 2, 4
BF = jnp.bfloat16
F32 = jnp.float32

LEN = (1536, 1536, 4608, 2560)
NB = 4


def dot(a, b, ca=1, cb=0):
    return lax.dot_general(a, b, (((ca,), (cb,)), ((), ())), preferred_element_type=F32)


def normalize(values):
    mean = jnp.mean(values, axis=-1, keepdims=True)
    centred = values - mean
    spread = jnp.mean(centred * centred, axis=-1, keepdims=True)
    return centred * lax.rsqrt(spread + EPSILON)


def onehot(mask):
    return mask.astype(F32).astype(BF)


def softmax0(logits):
    top = jnp.max(logits, axis=0, keepdims=True)
    e = jnp.exp(logits - top)
    return e / jnp.sum(e, axis=0, keepdims=True)


def rows(start, size):
    return pl.ds(pl.multiple_of(start, 16), size)


def lanes(start, size):
    return pl.ds(pl.multiple_of(start, 128), size)


def kernel(
    pview, rview, patches, rays, targets, slots_init, camera,
    wq, wk, wv, mk, gi, gh, mq, rin_w, rout,
    slots_out, colour_out, loss_out, gin_out, gro_out,
    cy0, cy1, cy2, cy3, f0, f1, f2, f3, sg0, sg1, sg2, sg3, rp, camsg, camcy, camf,
    px, rin, rx, ro, state, tsend, trecv, tysend, tyrecv, tzsend, tzrecv,
    psend, precv, ssend, srecv, dcol8, small, smrecv_cx, smrecv_y, smrecv_z, smy, smz,
    jt, gown, gcs, gcr, gxs, gxr, gzs, gzr, gys, gyr, gfs, gfr,
    cy_s, cy_r, z_s, z_r, x_s, x_r, c_s, c_r, it_s, it_r, gr_s, gr_r, gc_s, gc_r, gx_s, gx_r,
):
    z, y, c, x = (lax.axis_index(a) for a in ("z", "y", "c", "x"))
    cyb, full, stage = (cy0, cy1, cy2, cy3), (f0, f1, f2, f3), (sg0, sg1, sg2, sg3)
    width = patches.shape[1]
    scale = width ** (-0.5)
    pending = []

    def send(src, dst, ssem, rsem, **where):
        cp = pltpu.make_async_remote_copy(
            src_ref=src, dst_ref=dst, send_sem=ssem, recv_sem=rsem,
            device_id=where, device_id_type=pl.DeviceIdType.MESH,
        )
        cp.start()
        pending.append(cp)
        return cp

    def yc_peers():
        return [(dy, dc) for dy in range(NY) for dc in range(NC) if dy or dc]

    def cx_peers():
        return [(dc, dx) for dc in range(NC) for dx in range(NX) if dc or dx]

    def flip(dc):
        return 1 - c if dc else c

    barrier = pltpu.get_barrier_semaphore()
    met = 0
    for dy, dc in yc_peers():
        pl.semaphore_signal(barrier, inc=1, device_id={"y": lax.rem(y + dy, NY), "c": flip(dc)}, device_id_type=pl.DeviceIdType.MESH)
        met += 1
    for dc, dx in cx_peers():
        if dx:
            pl.semaphore_signal(barrier, inc=1, device_id={"x": lax.rem(x + dx, NX), "c": flip(dc)}, device_id_type=pl.DeviceIdType.MESH)
            met += 1
    for dz in range(1, NZ):
        pl.semaphore_signal(barrier, inc=1, device_id={"z": lax.rem(z + dz, NZ)}, device_id_type=pl.DeviceIdType.MESH)
        met += 1
    pl.semaphore_wait(barrier, met)

    me_yc = y * 2 + c
    quarter = x * (1 - c) + y * c

    def along(d):
        return dict(x=lax.rem(x + d * (1 - c), NX), y=lax.rem(y + d * c, NY))

    def across(d):
        return dict(x=lax.rem(x + d * c, NX), y=lax.rem(y + d * (1 - c), NY))

    def yc_copies(src, buf, slot, w, part):
        out = []
        for k, (dy, dc) in enumerate(yc_peers()):
            yy, cc = lax.rem(y + dy, NY), flip(dc)
            cp = pltpu.make_async_remote_copy(
                src_ref=src.at[:, lanes(part(yy, cc) * w, w)], dst_ref=buf.at[rows(me_yc * 16, 16)],
                send_sem=cy_s.at[slot, k], recv_sem=cy_r.at[slot, k],
                device_id={"y": yy, "c": cc}, device_id_type=pl.DeviceIdType.MESH,
            )
            out.append((cp, dy, cc))
        return out

    def pack(b, parts):
        stage[b][...] = jnp.zeros_like(stage[b])
        at = 0
        for part in parts:
            stage[b][0:12, at : at + part.shape[1]] = part[...]
            at += part.shape[1]

    def pack_colour(at):
        rp[...] = jnp.zeros_like(rp)
        rp[0:3, :] = rout[...].astype(F32)
        unit = lax.broadcasted_iota(jnp.int32, (16, 24), 1)
        row = lax.broadcasted_iota(jnp.int32, (16, 24), 0)
        for j in range(2):
            mask = (unit == row + 12 * j) & (row < 12)
            stage[3][:, at + 128 * j : at + 128 * j + 128] = dot(onehot(mask), rp[...].astype(BF), 1, 1).astype(BF)

    def start_bundle(b):
        w = LEN[b] // NX
        cyb[b][rows(me_yc * 16, 16), :] = stage[b][:, lanes(quarter * w, w)]
        cps = yc_copies(stage[b], cyb[b], b, w, lambda yy, cc: x * (1 - cc) + yy * cc)
        for cp, dy, cc in cps:
            @pl.when(y // 2 == cc)
            def _():
                cp.start()

        return cps

    def finish_bundle(cps):
        for cp, dy, cc in cps:
            @pl.when(lax.rem(y - dy + NY, NY) // 2 == c)
            def _():
                cp.wait_recv()

            @pl.when(y // 2 == cc)
            def _():
                cp.wait_send()

    def compact(shards, real, first, count):
        n = shards.shape[0]
        r = lax.broadcasted_iota(jnp.int32, (count, n), 0) + first
        k = lax.broadcasted_iota(jnp.int32, (count, n), 1)
        lane = k % 16
        mask = (lane < real) & (r == (k // 16) * real + lane)
        return dot(onehot(mask), shards).astype(BF)

    def piece(b, zz):
        w = LEN[b] // NX
        return full[b].at[rows(zz * 96 + c * 48, 48), lanes(quarter * w, w)]

    def start_z(b, arrived, ring=True):
        finish_bundle(arrived)
        w = LEN[b] // NX
        full[b][rows(z * 96 + c * 48, 48), lanes(quarter * w, w)] = compact(cyb[b][rows(c * 64, 64), :], 12, 0, 48)
        if not ring:
            return [
                send(piece(b, z), piece(b, z), z_s.at[b, d], z_r.at[b, d], z=lax.rem(z + d, NZ))
                for d in range(1, NZ)
            ]
        return [pass_on(b, z, 1), pass_on(b, z, NZ - 1)]

    def pass_on(b, zz, d):
        to = lax.rem(z + (1 if d <= NZ // 2 else NZ - 1), NZ)
        return send(piece(b, zz), piece(b, zz), z_s.at[b, d], z_r.at[b, d], z=to)

    def forward_x(b, ref, d):
        return [send(ref, ref, x_s.at[b, k, d], x_r.at[b, k, d], **along(k)) for k in range(1, NX)]

    def ring_x(bundles):
        out = {b: [(0, forward_x(b, piece(b, z), 0))] for b, _ in bundles}
        sent = {b: list(first) for b, first in bundles}
        for k in range(1, NZ // 2 + 1):
            for d in (k, NZ - k) if k < NZ // 2 else (k,):
                for b, _ in bundles:
                    zz = lax.rem(z - d + NZ, NZ)
                    pltpu.make_async_remote_copy(
                        src_ref=piece(b, zz), dst_ref=piece(b, zz), send_sem=z_s.at[b, d], recv_sem=z_r.at[b, d],
                        device_id={"z": zz}, device_id_type=pl.DeviceIdType.MESH,
                    ).wait_recv()
                    if d < NZ // 2:
                        sent[b].append(pass_on(b, zz, d + 1))
                    if d > NZ // 2 + 1:
                        sent[b].append(pass_on(b, zz, d - 1))
                    out[b].append((d, forward_x(b, piece(b, zz), d)))
        return {b: (out[b], sent[b]) for b, _ in bundles}

    def swap_core(b, gathered):
        arriving, sent = gathered
        for cp in sent:
            cp.wait_send()
        cps = []
        for d, group_cps in arriving:
            for cp in group_cps:
                cp.wait()
            ref = full[b].at[rows(lax.rem(z - d + NZ, NZ) * 96 + c * 48, 48)]
            cps.append(send(ref, ref, c_s.at[b, d], c_r.at[b, d], c=1 - c))
        return cps

    def done(cps):
        for cp in cps:
            cp.wait()

    half = width // 2
    pack(0, (wq, wk))
    cy_b0 = start_bundle(0)
    camsg[...] = jnp.zeros_like(camsg)
    camsg[0:8, :] = camera[...]
    camcy[rows(me_yc * 16, 16), :] = camsg[:, lanes(c * half, half)]
    cy_cam = yc_copies(camsg, camcy, 4, half, lambda yy, cc: cc)
    for cp, _, _ in cy_cam:
        cp.start()
    n0 = normalize(slots_init[...]).astype(BF)
    z_b0 = start_z(0, cy_b0)
    for cp, _, _ in cy_cam:
        cp.wait()
    camf[rows(z * 64 + quarter * 16, 16), lanes(c * half, half)] = compact(camcy[...], 8, quarter * 16, 16)

    def cam_piece(zz):
        return camf.at[rows(zz * 64 + quarter * 16, 16), lanes(c * half, half)]

    z_cam = [
        send(cam_piece(z), cam_piece(z), z_s.at[4, d], z_r.at[4, d], z=lax.rem(z + d, NZ))
        for d in range(1, NZ)
    ]
    pack(1, (wv, mk))
    cy_b1 = start_bundle(1)
    pack(2, (gi, gh))
    cy_b2 = start_bundle(2)
    x_b0 = ring_x([(0, z_b0)])[0]
    z_b1 = start_z(1, cy_b1)
    z_b2 = start_z(2, cy_b2)
    x_cam = forward_x(4, cam_piece(z), 0)
    for d in range(1, NZ):
        z_cam[d - 1].wait()
        x_cam += forward_x(4, cam_piece(lax.rem(z - d + NZ, NZ)), d)
    pack(3, (mq, rin_w))
    pack_colour(3 * width)
    cy_b3 = start_bundle(3)
    c_b0 = swap_core(0, x_b0)
    bulk = ring_x([(1, z_b1), (2, z_b2)])
    z_b3 = start_z(3, cy_b3, ring=False)
    done(x_cam)
    cam_half = camf.at[:, lanes(c * half, half)]
    done([send(cam_half, cam_half, c_s.at[4, 0], c_r.at[4, 0], c=1 - c)])

    def lookup(view):
        v = lax.broadcasted_iota(jnp.int32, (camf.shape[0], view.shape[1]), 0)
        return dot(onehot(v == view[...]), camf[...], 0, 0)

    px[...] = normalize(patches[...].astype(F32) + lookup(pview)).astype(BF)
    rin[...] = rays[...].astype(F32) + lookup(rview)
    rx[...] = rin[...].astype(BF)
    done(c_b0)

    def slot_projection(normed):
        query = (dot(normed, f0[:, 0:width]) * scale).astype(BF)
        return dot(query, f0[:, width : 2 * width], 1, 1).astype(BF)

    group = c * NX + x
    mine = pl.ds(pl.multiple_of(group * 8, 8), 8)
    state[...] = slots_init[mine, :]
    proj = slot_projection(n0)
    x_b3, c_b3 = [], []
    gaps = ((0, 1, 2), (3, 4, 5), (6, 7))

    def group_rows(buf, t):
        return jnp.concatenate([buf[t, g].astype(F32) for g in range(8)], axis=0)

    def share(t, value):
        psend[t] = value
        precv[t, group] = value
        return [
            send(psend.at[t], precv.at[t, group], it_s.at[t, 24 + k], it_r.at[t, 24 + k],
                 c=flip(dc), x=lax.rem(x + dx, NX))
            for k, (dc, dx) in enumerate(cx_peers())
        ]

    for t in range(ITERS):
        attn = softmax0(dot(proj, px[...], 1, 1)) + ATTN_FLOOR
        total = dot(attn.astype(BF), px[...])
        denom = jnp.sum(attn, axis=1, keepdims=True)
        for g in range(8):
            tsend[t, g, :, 0:width] = total[8 * g : 8 * g + 8].astype(BF)
            tsend[t, g, :, width : width + 128] = jnp.broadcast_to(denom[8 * g : 8 * g + 8], (8, 128)).astype(BF)
        cps = []
        for k, (dc, dx) in enumerate(cx_peers()):
            cc, xx = flip(dc), lax.rem(x + dx, NX)
            cps.append(send(tsend.at[t, cc * NX + xx], trecv.at[t, k], it_s.at[t, k], it_r.at[t, k], c=cc, x=xx))
        acc = tsend[t, group].astype(F32)
        for k, cp in enumerate(cps):
            cp.wait()
            acc += trecv[t, k].astype(F32)
        tysend[t] = acc.astype(BF)
        cps = [
            send(tysend.at[t], tyrecv.at[t, d], it_s.at[t, 8 + d], it_r.at[t, 8 + d], y=lax.rem(y + d, NY))
            for d in range(1, NY)
        ]
        for cp in cps:
            cp.wait()
        acc = ordered(tyrecv, tysend, t, y, NY)
        tzsend[t] = acc.astype(BF)
        cps = [
            send(tzsend.at[t], tzrecv.at[t, d], it_s.at[t, 12 + d], it_r.at[t, 12 + d], z=lax.rem(z + d, NZ))
            for d in range(1, NZ)
        ]
        if t == 0:
            c_b1 = swap_core(1, bulk[1])
            c_b2 = swap_core(2, bulk[2])
        if t:
            c_b3 += swap_core(3, (x_b3, []))
            x_b3 = []
        for d in gaps[t]:
            if d:
                z_b3[d - 1].wait()
            x_b3.append((d, forward_x(3, piece(3, lax.rem(z - d + NZ, NZ)), d)))
        for cp in cps:
            cp.wait()
        acc = ordered(tzrecv, tzsend, t, z, NZ)
        if t == 0:
            done(c_b1)
            done(c_b2)
        mean_x = (acc[:, 0:width] / acc[:, width : width + 1]).astype(BF)
        update = dot(mean_x, f1[:, 0:width]).astype(BF)
        slots = state[...]
        a = dot(update, f2[:, 0 : 3 * width])
        b = dot(slots.astype(BF), f2[:, 3 * width : 6 * width])
        reset = jax.nn.sigmoid(a[:, 0:width] + b[:, 0:width])
        blend = jax.nn.sigmoid(a[:, width : 2 * width] + b[:, width : 2 * width])
        cand = jnp.tanh(a[:, 2 * width :] + reset * b[:, 2 * width :])
        slots = (1.0 - blend) * cand + blend * slots
        state[...] = slots
        if t + 1 < ITERS:
            cps = share(t, slot_projection(normalize(slots).astype(BF)))
            done(cps)
            proj = group_rows(precv, t).astype(BF)

    t = ITERS - 1
    ssend[...] = slots
    srecv[mine, :] = slots
    s_cps = [
        send(ssend, srecv.at[mine], gr_s.at[0, k], gr_r.at[0, k], c=flip(dc), x=lax.rem(x + dx, NX))
        for k, (dc, dx) in enumerate(cx_peers())
    ]
    done(c_b3 + swap_core(3, (x_b3, [])))
    slot_keys = dot(slots.astype(BF), f1[:, width : 2 * width]).astype(BF)
    r_cps = share(t, (dot(slot_keys, f3[:, 0:width], 1, 1) * scale).astype(BF))
    r = lax.broadcasted_iota(jnp.int32, (width, 1), 0)
    hid = 2 * r - r % 12
    unit = lax.broadcasted_iota(jnp.int32, (width, 2 * width), 1)
    ro[...] = (
        dot(f3[:, 3 * width : 3 * width + 128], onehot(unit == hid), 0, 0)
        + dot(f3[:, 3 * width + 128 : 3 * width + 256], onehot(unit == hid + 12), 0, 0)
    )[0:8].astype(BF)
    done(s_cps)
    done(r_cps)
    slots_all = srecv[...]
    slots_out[...] = slots_all
    low = slots_all.astype(BF)
    mix = softmax0(dot(group_rows(precv, t).astype(BF), rx[...], 1, 1)).astype(BF)
    joined = (dot(mix, low, 0, 0) + rin[...]).astype(BF)
    pre = dot(joined, f3[:, width : 3 * width])
    sig = jax.nn.sigmoid(pre)
    hidden = (pre * sig).astype(BF)
    colour = dot(ro[...], hidden, 1, 1)[0:3]
    colour_out[...] = colour
    error = colour - targets[...]
    rays_total = rin.shape[0] * NZ * NY * NC * NX
    dcol8[...] = jnp.zeros_like(dcol8)
    dcol8[0:3, :] = error * (2.0 / jnp.sqrt(jnp.float32(3.0 * rays_total)))
    dcol = dcol8[...].astype(BF)
    dpre = (dot(dcol, ro[...], 0, 0) * (sig + pre * sig * (1.0 - sig))).astype(BF)
    gro = dot(dcol, hidden)
    squared = jnp.sum(jnp.sum(error * error, axis=1, keepdims=True), axis=0, keepdims=True)

    turned = jnp.transpose(joined.astype(F32)).astype(BF)
    for zz in range(NZ):
        for h in range(NC):
            jt[384 * h + 48 * zz : 384 * h + 48 * zz + 48, :] = turned[96 * zz + 48 * h : 96 * zz + 48 * h + 48]
    order = (4, 3, 5, 2, 6, 1, 7, 0)

    def block(d):
        return rows(lax.rem(z + d, NZ) * 48, 48)

    gcs[...] = dot(jt[rows(384 * (1 - c), 384), :], dpre).astype(BF)
    g_c = {d: send(gcs.at[block(d)], gcr.at[block(d)], gc_s.at[d], gc_r.at[d], c=1 - c) for d in order}
    small[...] = jnp.zeros_like(small)
    small[0:3, :] = gro[0:3, 0:width]
    small[3:6, :] = gro[0:3, width:]
    small[6:7, :] = jnp.broadcast_to(squared, (1, width))
    sm_cps = [
        send(small, smrecv_cx.at[group], gr_s.at[2, k], gr_r.at[2, k], c=flip(dc), x=lax.rem(x + dx, NX))
        for k, (dc, dx) in enumerate(cx_peers())
    ]
    smrecv_cx[group] = small[...]
    gown[...] = dot(jt[rows(384 * c, 384), :], dpre)
    qw = 2 * width // NX
    gx = {}
    for d in order:
        g_c[d].wait()
        gsum = gown[block(d), :] + gcr[block(d), :].astype(F32)
        gown[block(d), :] = gsum
        gxs[block(d), :] = gsum.astype(BF)
        gx[d] = [
            send(gxs.at[block(d), lanes(lax.rem(quarter + k, NX) * qw, qw)], gxr.at[k, block(d)],
                 gx_s.at[k, d], gx_r.at[k, d], **along(k))
            for k in range(1, NX)
        ]
    done(sm_cps)
    acc_s = sum_of(smrecv_cx, 8)
    smy[...] = acc_s
    smrecv_y[y] = acc_s
    sm_cps = [
        send(smy, smrecv_y.at[y], gr_s.at[4, d], gr_r.at[4, d], y=lax.rem(y + d, NY)) for d in range(1, NY)
    ]
    gz = []
    for d in order:
        done(gx[d])
        acc_g = gown[block(d), lanes(quarter * qw, qw)]
        for k in range(1, NX):
            acc_g += gxr[k, block(d), :].astype(F32)
        gzs[block(d), :] = acc_g.astype(BF)
        if d:
            gz.append((d, send(gzs.at[block(d)], gzr.at[d], gr_s.at[6, d], gr_r.at[6, d], z=lax.rem(z + d, NZ))))
    done(sm_cps)
    acc_s = sum_of(smrecv_y, NY)
    smz[...] = acc_s
    smrecv_z[z] = acc_s
    sm_cps = [
        send(smz, smrecv_z.at[z], gr_s.at[5, d], gr_r.at[5, d], z=lax.rem(z + d, NZ)) for d in range(1, NZ)
    ]
    for d, cp in gz:
        cp.wait()
        acc_g += gzr[d].astype(F32)
    gys[0] = acc_g.astype(BF)
    g_b = [send(gys.at[0], gyr.at[0, d], gr_s.at[7, d], gr_r.at[7, d], **across(d)) for d in range(1, NY)]
    done(sm_cps)
    acc_s = sum_of(smrecv_z, NZ)
    gro_out[:, 0:width] = acc_s[0:3]
    gro_out[:, width:] = acc_s[3:6]
    loss_out[...] = acc_s[6:7, 0:1] / (3.0 * rays_total)
    done(g_b)
    place = x * c + y * (1 - c)
    gfs[...] = ordered(gyr, gys, 0, place, NY)

    def final(k, row, slot, **where):
        return pltpu.make_async_remote_copy(
            src_ref=gfs.at[pl.ds(pl.multiple_of(row * 24, 8), 24)], dst_ref=gfr.at[slot],
            send_sem=gr_s.at[8, k], recv_sem=gr_r.at[8, slot],
            device_id=where, device_id_type=pl.DeviceIdType.MESH,
        )

    low_half = y // 2 == 0
    keeps = y // 2 == c
    own_row = lax.rem(y, 2)

    @pl.when(keeps)
    def _():
        gfr[quarter] = gfs[pl.ds(pl.multiple_of(own_row * 24, 8), 24), :]

    def to_x(act):
        for k, (dc, dx) in enumerate(cx_peers()):
            act(final(k, own_row, quarter, c=flip(dc), x=lax.rem(x + dx, NX)))

    def to_y(act):
        for k in range(4):
            yy, cc = 2 + k // 2, k % 2

            @pl.when(jnp.logical_not((y == yy) & (c == cc)))
            def _():
                act(final(k, k // 2, quarter, y=yy, c=cc))

    @pl.when((c == 0) & low_half)
    def _():
        to_x(lambda cp: cp.start())

    @pl.when(c == 1)
    def _():
        to_y(lambda cp: cp.start())

    for slot in range(NX):
        @pl.when(jnp.logical_not(keeps & (quarter == slot)))
        def _():
            final(0, 0, slot, c=1 - c).wait_recv()

        blk = gfr[slot]
        gin_out[:, qw * slot : qw * slot + qw] = jnp.where(c == 0, blk[0:12], blk[12:24])

    @pl.when((c == 0) & low_half)
    def _():
        to_x(lambda cp: cp.wait_send())

    @pl.when(c == 1)
    def _():
        to_y(lambda cp: cp.wait_send())


def sum_of(buf, n):
    acc = buf[0]
    for j in range(1, n):
        acc += buf[j]
    return acc


def ordered(recv, own, t, me, n):
    acc = None
    for j in range(n):
        d = lax.rem(me - j + n, n)
        val = jnp.where(d == 0, own[t].astype(F32), recv[t, d].astype(F32))
        acc = val if acc is None else acc + val
    return acc


def on_device(
    patches, patch_view, rays, ray_view, targets, camera, slots_init, key_weight, value_weight,
    query_weight, gru_input, gru_hidden, mix_query, mix_key, render_in, render_out,
):
    n, width = patches.shape
    V, S = pltpu.VMEM, pltpu.SemaphoreType.DMA
    vm = pl.BlockSpec(memory_space=pltpu.VMEM)
    scratch = (
        [V((128, L // NX), BF) for L in LEN]
        + [V((width, L), BF) for L in LEN]
        + [V((16, L), BF) for L in LEN]
        + [
            V((128, 24), F32), V((16, width), BF), V((128, width // 2), BF), V((512, width), BF),
            V((n, width), BF), V((n, width), F32), V((n, width), BF), V((8, 2 * width), BF), V((8, width), F32),
            V((3, 8, 8, width + 128), BF), V((3, 8, 8, width + 128), BF),
            V((3, 8, width + 128), BF), V((3, NY, 8, width + 128), BF),
            V((3, 8, width + 128), BF), V((3, NZ, 8, width + 128), BF),
            V((3, 8, width), BF), V((3, 8, 8, width), BF), V((8, width), F32), V((64, width), F32),
            V((8, n), F32), V((8, width), F32), V((8, 8, width), F32), V((NY, 8, width), F32), V((NZ, 8, width), F32),
            V((8, width), F32), V((8, width), F32),
            V((width, n), BF), V((384, 2 * width), F32), V((384, 2 * width), BF), V((384, 2 * width), BF),
            V((384, 2 * width), BF), V((NX, 384, width // 2), BF), V((384, width // 2), BF), V((NZ, 48, width // 2), BF),
            V((1, 48, width // 2), BF), V((1, NY, 48, width // 2), BF), V((48, width // 2), F32), V((NX, 24, width // 2), F32),
            S((5, 7)), S((5, 7)), S((5, 8)), S((5, 8)), S((5, 4, 8)), S((5, 4, 8)), S((5, 8)), S((5, 8)),
            S((3, 32)), S((3, 32)), S((9, 8)), S((9, 8)), S((8,)), S((8,)), S((4, 8)), S((4, 8)),
        ]
    )
    out = pl.pallas_call(
        kernel,
        out_shape=[
            jax.ShapeDtypeStruct((64, width), F32),
            jax.ShapeDtypeStruct((3, n), F32),
            jax.ShapeDtypeStruct((1, 1), F32),
            jax.ShapeDtypeStruct((12, 2 * width), F32),
            jax.ShapeDtypeStruct((3, 2 * width), F32),
        ],
        in_specs=[vm] * 16,
        out_specs=[vm] * 5,
        scratch_shapes=scratch,
        compiler_params=pltpu.CompilerParams(collective_id=0, has_side_effects=True, vmem_limit_bytes=60 << 20),
    )(
        patch_view[None], ray_view[None], patches, rays, targets, slots_init, camera, query_weight, key_weight,
        value_weight, mix_key, gru_input, gru_hidden, mix_query, render_in, render_out,
    )
    slots, colour, loss, gin, gro = out
    return slots, colour, loss[0, 0], gin, gro


def solution(mesh):
    torus = Mesh(mesh.devices.reshape(NZ, NY, NC, NX), ("z", "y", "c", "x"))
    tok, every = ("z", "y", "c"), ("z", "y", "c", "x")
    w = P(tok, None)
    return jax.shard_map(
        on_device,
        mesh=torus,
        in_specs=(
            P(every, None), P(every), P(every, None), P(every), P(None, every), w, P(),
            w, w, w, w, w, w, w, w, P(None, tok),
        ),
        out_specs=(P(), P(None, every), P(), w, P()),
        check_vma=False,
    )
```

```python
import functools

import jax
import jax.numpy as jnp
from jax import lax
from jax.experimental import pallas as pl
from jax.experimental.pallas import tpu as pltpu
from jax.sharding import Mesh
from jax.sharding import PartitionSpec as P

ITERS = 3
EPSILON = 1e-05
ATTN_FLOOR = 1e-08
NZ, NY, NC, NX = 8, 4, 2, 4
BF = jnp.bfloat16
F32 = jnp.float32

LEN = (1536, 1536, 4608, 2560)
NB = 4


def dot(a, b, ca=1, cb=0):
    return lax.dot_general(a, b, (((ca,), (cb,)), ((), ())), preferred_element_type=F32)


def normalize(values):
    mean = jnp.mean(values, axis=-1, keepdims=True)
    centred = values - mean
    spread = jnp.mean(centred * centred, axis=-1, keepdims=True)
    return centred * lax.rsqrt(spread + EPSILON)


def onehot(mask):
    return mask.astype(F32).astype(BF)


def softmax0(logits):
    top = jnp.max(logits, axis=0, keepdims=True)
    e = jnp.exp(logits - top)
    return e / jnp.sum(e, axis=0, keepdims=True)


def rows(start, size):
    return pl.ds(pl.multiple_of(start, 16), size)


def lanes(start, size):
    return pl.ds(pl.multiple_of(start, 128), size)


def kernel(
    pview, rview, patches, rays, targets, slots_init, camera,
    wq, wk, wv, mk, gi, gh, mq, rin_w, rout,
    slots_out, colour_out, loss_out, gin_out, gro_out,
    cy0, cy1, cy2, cy3, f0, f1, f2, f3, sg0, sg1, sg2, sg3, rp, camsg, camcy, camf,
    px, rin, rx, ro, state, tsend, trecv, tysend, tyrecv, tzsend, tzrecv,
    psend, precv, ssend, srecv, dcol8, small, smrecv_cx, smrecv_y, smrecv_z, smy, smz,
    jt, gown, gcs, gcr, gxs, gxr, gzs, gzr, gys, gyr, gfs, gfr,
    cy_s, cy_r, z_s, z_r, x_s, x_r, c_s, c_r, it_s, it_r, gr_s, gr_r, gc_s, gc_r, gx_s, gx_r,
):
    z, y, c, x = (lax.axis_index(a) for a in ("z", "y", "c", "x"))
    cyb, full, stage = (cy0, cy1, cy2, cy3), (f0, f1, f2, f3), (sg0, sg1, sg2, sg3)
    width = patches.shape[1]
    scale = width ** (-0.5)
    pending = []

    def send(src, dst, ssem, rsem, **where):
        cp = pltpu.make_async_remote_copy(
            src_ref=src, dst_ref=dst, send_sem=ssem, recv_sem=rsem,
            device_id=where, device_id_type=pl.DeviceIdType.MESH,
        )
        cp.start()
        pending.append(cp)
        return cp

    def yc_peers():
        return [(dy, dc) for dy in range(NY) for dc in range(NC) if dy or dc]

    def cx_peers():
        return [(dc, dx) for dc in range(NC) for dx in range(NX) if dc or dx]

    def flip(dc):
        return 1 - c if dc else c

    barrier = pltpu.get_barrier_semaphore()
    met = 0
    for dy, dc in yc_peers():
        pl.semaphore_signal(barrier, inc=1, device_id={"y": lax.rem(y + dy, NY), "c": flip(dc)}, device_id_type=pl.DeviceIdType.MESH)
        met += 1
    for dc, dx in cx_peers():
        if dx:
            pl.semaphore_signal(barrier, inc=1, device_id={"x": lax.rem(x + dx, NX), "c": flip(dc)}, device_id_type=pl.DeviceIdType.MESH)
            met += 1
    for dz in range(1, NZ):
        pl.semaphore_signal(barrier, inc=1, device_id={"z": lax.rem(z + dz, NZ)}, device_id_type=pl.DeviceIdType.MESH)
        met += 1
    pl.semaphore_wait(barrier, met)

    me_yc = y * 2 + c
    quarter = x * (1 - c) + y * c

    def along(d):
        return dict(x=lax.rem(x + d * (1 - c), NX), y=lax.rem(y + d * c, NY))

    def across(d):
        return dict(x=lax.rem(x + d * c, NX), y=lax.rem(y + d * (1 - c), NY))

    def yc_copies(src, buf, slot, w, part):
        out = []
        for k, (dy, dc) in enumerate(yc_peers()):
            yy, cc = lax.rem(y + dy, NY), flip(dc)
            cp = pltpu.make_async_remote_copy(
                src_ref=src.at[:, lanes(part(yy, cc) * w, w)], dst_ref=buf.at[rows(me_yc * 16, 16)],
                send_sem=cy_s.at[slot, k], recv_sem=cy_r.at[slot, k],
                device_id={"y": yy, "c": cc}, device_id_type=pl.DeviceIdType.MESH,
            )
            out.append((cp, dy, cc))
        return out

    def pack(b, parts):
        stage[b][...] = jnp.zeros_like(stage[b])
        at = 0
        for part in parts:
            stage[b][0:12, at : at + part.shape[1]] = part[...]
            at += part.shape[1]

    def pack_colour(at):
        rp[...] = jnp.zeros_like(rp)
        rp[0:3, :] = rout[...].astype(F32)
        unit = lax.broadcasted_iota(jnp.int32, (16, 24), 1)
        row = lax.broadcasted_iota(jnp.int32, (16, 24), 0)
        for j in range(2):
            mask = (unit == row + 12 * j) & (row < 12)
            stage[3][:, at + 128 * j : at + 128 * j + 128] = dot(onehot(mask), rp[...].astype(BF), 1, 1).astype(BF)

    def start_bundle(b):
        w = LEN[b] // NX
        cyb[b][rows(me_yc * 16, 16), :] = stage[b][:, lanes(quarter * w, w)]
        cps = yc_copies(stage[b], cyb[b], b, w, lambda yy, cc: x * (1 - cc) + yy * cc)
        for cp, dy, cc in cps:
            @pl.when(y // 2 == cc)
            def _():
                cp.start()

        return cps

    def finish_bundle(cps):
        for cp, dy, cc in cps:
            @pl.when(lax.rem(y - dy + NY, NY) // 2 == c)
            def _():
                cp.wait_recv()

            @pl.when(y // 2 == cc)
            def _():
                cp.wait_send()

    def compact(shards, real, first, count):
        n = shards.shape[0]
        r = lax.broadcasted_iota(jnp.int32, (count, n), 0) + first
        k = lax.broadcasted_iota(jnp.int32, (count, n), 1)
        lane = k % 16
        mask = (lane < real) & (r == (k // 16) * real + lane)
        return dot(onehot(mask), shards).astype(BF)

    def piece(b, zz):
        w = LEN[b] // NX
        return full[b].at[rows(zz * 96 + c * 48, 48), lanes(quarter * w, w)]

    def start_z(b, arrived, ring=True):
        finish_bundle(arrived)
        w = LEN[b] // NX
        full[b][rows(z * 96 + c * 48, 48), lanes(quarter * w, w)] = compact(cyb[b][rows(c * 64, 64), :], 12, 0, 48)
        if not ring:
            return [
                send(piece(b, z), piece(b, z), z_s.at[b, d], z_r.at[b, d], z=lax.rem(z + d, NZ))
                for d in range(1, NZ)
            ]
        return [pass_on(b, z, 1), pass_on(b, z, NZ - 1)]

    def pass_on(b, zz, d):
        to = lax.rem(z + (1 if d <= NZ // 2 else NZ - 1), NZ)
        return send(piece(b, zz), piece(b, zz), z_s.at[b, d], z_r.at[b, d], z=to)

    def forward_x(b, ref, d):
        return [send(ref, ref, x_s.at[b, k, d], x_r.at[b, k, d], **along(k)) for k in range(1, NX)]

    def ring_x(bundles):
        out = {b: [(0, forward_x(b, piece(b, z), 0))] for b, _ in bundles}
        sent = {b: list(first) for b, first in bundles}
        for k in range(1, NZ // 2 + 1):
            for d in (k, NZ - k) if k < NZ // 2 else (k,):
                for b, _ in bundles:
                    zz = lax.rem(z - d + NZ, NZ)
                    pltpu.make_async_remote_copy(
                        src_ref=piece(b, zz), dst_ref=piece(b, zz), send_sem=z_s.at[b, d], recv_sem=z_r.at[b, d],
                        device_id={"z": zz}, device_id_type=pl.DeviceIdType.MESH,
                    ).wait_recv()
                    if d < NZ // 2:
                        sent[b].append(pass_on(b, zz, d + 1))
                    if d > NZ // 2 + 1:
                        sent[b].append(pass_on(b, zz, d - 1))
                    out[b].append((d, forward_x(b, piece(b, zz), d)))
        return {b: (out[b], sent[b]) for b, _ in bundles}

    def swap_core(b, gathered):
        arriving, sent = gathered
        for cp in sent:
            cp.wait_send()
        cps = []
        for d, group_cps in arriving:
            for cp in group_cps:
                cp.wait()
            ref = full[b].at[rows(lax.rem(z - d + NZ, NZ) * 96 + c * 48, 48)]
            cps.append(send(ref, ref, c_s.at[b, d], c_r.at[b, d], c=1 - c))
        return cps

    def done(cps):
        for cp in cps:
            cp.wait()

    half = width // 2
    pack(0, (wq, wk))
    cy_b0 = start_bundle(0)
    camsg[...] = jnp.zeros_like(camsg)
    camsg[0:8, :] = camera[...]
    camcy[rows(me_yc * 16, 16), :] = camsg[:, lanes(c * half, half)]
    cy_cam = yc_copies(camsg, camcy, 4, half, lambda yy, cc: cc)
    for cp, _, _ in cy_cam:
        cp.start()
    n0 = normalize(slots_init[...]).astype(BF)
    z_b0 = start_z(0, cy_b0)
    for cp, _, _ in cy_cam:
        cp.wait()
    camf[rows(z * 64 + quarter * 16, 16), lanes(c * half, half)] = compact(camcy[...], 8, quarter * 16, 16)

    def cam_piece(zz):
        return camf.at[rows(zz * 64 + quarter * 16, 16), lanes(c * half, half)]

    z_cam = [
        send(cam_piece(z), cam_piece(z), z_s.at[4, d], z_r.at[4, d], z=lax.rem(z + d, NZ))
        for d in range(1, NZ)
    ]
    pack(1, (wv, mk))
    cy_b1 = start_bundle(1)
    pack(2, (gi, gh))
    cy_b2 = start_bundle(2)
    x_b0 = ring_x([(0, z_b0)])[0]
    z_b1 = start_z(1, cy_b1)
    z_b2 = start_z(2, cy_b2)
    x_cam = forward_x(4, cam_piece(z), 0)
    for d in range(1, NZ):
        z_cam[d - 1].wait()
        x_cam += forward_x(4, cam_piece(lax.rem(z - d + NZ, NZ)), d)
    pack(3, (mq, rin_w))
    pack_colour(3 * width)
    cy_b3 = start_bundle(3)
    c_b0 = swap_core(0, x_b0)
    done(x_cam)
    cam_half = camf.at[:, lanes(c * half, half)]
    done([send(cam_half, cam_half, c_s.at[4, 0], c_r.at[4, 0], c=1 - c)])

    def lookup(view):
        v = lax.broadcasted_iota(jnp.int32, (camf.shape[0], view.shape[1]), 0)
        return dot(onehot(v == view[...]), camf[...], 0, 0)

    px[...] = normalize(patches[...].astype(F32) + lookup(pview)).astype(BF)
    done(c_b0)

    def slot_projection(normed):
        query = (dot(normed, f0[:, 0:width]) * scale).astype(BF)
        return dot(query, f0[:, width : 2 * width], 1, 1).astype(BF)

    group = c * NX + x
    mine = pl.ds(pl.multiple_of(group * 8, 8), 8)
    state[...] = slots_init[mine, :]
    proj = slot_projection(n0)
    x_b3, c_b3 = [], []
    gaps = ((0, 1, 2, 3), (4, 5, 6, 7), ())

    def group_rows(buf, t):
        return jnp.concatenate([buf[t, g].astype(F32) for g in range(8)], axis=0)

    def share(t, value):
        psend[t] = value
        precv[t, group] = value
        return [
            send(psend.at[t], precv.at[t, group], it_s.at[t, 24 + k], it_r.at[t, 24 + k],
                 c=flip(dc), x=lax.rem(x + dx, NX))
            for k, (dc, dx) in enumerate(cx_peers())
        ]

    for t in range(ITERS):
        attn = softmax0(dot(proj, px[...], 1, 1)) + ATTN_FLOOR
        total = dot(attn.astype(BF), px[...])
        denom = jnp.sum(attn, axis=1, keepdims=True)
        for g in range(8):
            tsend[t, g, :, 0:width] = total[8 * g : 8 * g + 8].astype(BF)
            tsend[t, g, :, width : width + 128] = jnp.broadcast_to(denom[8 * g : 8 * g + 8], (8, 128)).astype(BF)
        cps = []
        for k, (dc, dx) in enumerate(cx_peers()):
            cc, xx = flip(dc), lax.rem(x + dx, NX)
            cps.append(send(tsend.at[t, cc * NX + xx], trecv.at[t, k], it_s.at[t, k], it_r.at[t, k], c=cc, x=xx))
        if t == 0:
            bulk = ring_x([(1, z_b1), (2, z_b2)])
            z_b3 = start_z(3, cy_b3, ring=False)
        acc = tsend[t, group].astype(F32)
        for k, cp in enumerate(cps):
            cp.wait()
            acc += trecv[t, k].astype(F32)
        tysend[t] = acc.astype(BF)
        cps = [
            send(tysend.at[t], tyrecv.at[t, d], it_s.at[t, 8 + d], it_r.at[t, 8 + d], y=lax.rem(y + d, NY))
            for d in range(1, NY)
        ]
        for cp in cps:
            cp.wait()
        acc = ordered(tyrecv, tysend, t, y, NY)
        tzsend[t] = acc.astype(BF)
        cps = [
            send(tzsend.at[t], tzrecv.at[t, d], it_s.at[t, 12 + d], it_r.at[t, 12 + d], z=lax.rem(z + d, NZ))
            for d in range(1, NZ)
        ]
        if t == 0:
            c_b1 = swap_core(1, bulk[1])
            c_b2 = swap_core(2, bulk[2])
        if t:
            c_b3 += swap_core(3, (x_b3, []))
            x_b3 = []
        for d in gaps[t]:
            if d:
                z_b3[d - 1].wait()
            x_b3.append((d, forward_x(3, piece(3, lax.rem(z - d + NZ, NZ)), d)))
        if t == 1:
            rin[...] = rays[...].astype(F32) + lookup(rview)
            rx[...] = rin[...].astype(BF)
        if t == 2:
            done(c_b3)
            r = lax.broadcasted_iota(jnp.int32, (width, 1), 0)
            hid = 2 * r - r % 12
            unit = lax.broadcasted_iota(jnp.int32, (width, 2 * width), 1)
            ro[...] = (
                dot(f3[:, 3 * width : 3 * width + 128], onehot(unit == hid), 0, 0)
                + dot(f3[:, 3 * width + 128 : 3 * width + 256], onehot(unit == hid + 12), 0, 0)
            )[0:8].astype(BF)
        for cp in cps:
            cp.wait()
        acc = ordered(tzrecv, tzsend, t, z, NZ)
        if t == 0:
            done(c_b1)
            done(c_b2)
        mean_x = (acc[:, 0:width] / acc[:, width : width + 1]).astype(BF)
        update = dot(mean_x, f1[:, 0:width]).astype(BF)
        slots = state[...]
        a = dot(update, f2[:, 0 : 3 * width])
        b = dot(slots.astype(BF), f2[:, 3 * width : 6 * width])
        reset = jax.nn.sigmoid(a[:, 0:width] + b[:, 0:width])
        blend = jax.nn.sigmoid(a[:, width : 2 * width] + b[:, width : 2 * width])
        cand = jnp.tanh(a[:, 2 * width :] + reset * b[:, 2 * width :])
        slots = (1.0 - blend) * cand + blend * slots
        state[...] = slots
        if t + 1 < ITERS:
            cps = share(t, slot_projection(normalize(slots).astype(BF)))
            done(cps)
            proj = group_rows(precv, t).astype(BF)

    t = ITERS - 1
    ssend[...] = slots
    srecv[mine, :] = slots
    s_cps = [
        send(ssend, srecv.at[mine], gr_s.at[0, k], gr_r.at[0, k], c=flip(dc), x=lax.rem(x + dx, NX))
        for k, (dc, dx) in enumerate(cx_peers())
    ]
    slot_keys = dot(slots.astype(BF), f1[:, width : 2 * width]).astype(BF)
    r_cps = share(t, (dot(slot_keys, f3[:, 0:width], 1, 1) * scale).astype(BF))
    done(s_cps)
    done(r_cps)
    slots_all = srecv[...]
    slots_out[...] = slots_all
    low = slots_all.astype(BF)
    mix = softmax0(dot(group_rows(precv, t).astype(BF), rx[...], 1, 1)).astype(BF)
    joined = (dot(mix, low, 0, 0) + rin[...]).astype(BF)
    pre = dot(joined, f3[:, width : 3 * width])
    sig = jax.nn.sigmoid(pre)
    hidden = (pre * sig).astype(BF)
    colour = dot(ro[...], hidden, 1, 1)[0:3]
    colour_out[...] = colour
    error = colour - targets[...]
    rays_total = rin.shape[0] * NZ * NY * NC * NX
    dcol8[...] = jnp.zeros_like(dcol8)
    dcol8[0:3, :] = error * (2.0 / jnp.sqrt(jnp.float32(3.0 * rays_total)))
    dcol = dcol8[...].astype(BF)
    dpre = (dot(dcol, ro[...], 0, 0) * (sig + pre * sig * (1.0 - sig))).astype(BF)
    gro = dot(dcol, hidden)
    squared = jnp.sum(jnp.sum(error * error, axis=1, keepdims=True), axis=0, keepdims=True)

    turned = jnp.transpose(joined.astype(F32)).astype(BF)
    for zz in range(NZ):
        for h in range(NC):
            jt[384 * h + 48 * zz : 384 * h + 48 * zz + 48, :] = turned[96 * zz + 48 * h : 96 * zz + 48 * h + 48]
    order = (4, 3, 5, 2, 6, 1, 7, 0)

    def block(d):
        return rows(lax.rem(z + d, NZ) * 48, 48)

    gcs[...] = dot(jt[rows(384 * (1 - c), 384), :], dpre).astype(BF)
    g_c = {d: send(gcs.at[block(d)], gcr.at[block(d)], gc_s.at[d], gc_r.at[d], c=1 - c) for d in order}
    small[...] = jnp.zeros_like(small)
    small[0:3, :] = gro[0:3, 0:width]
    small[3:6, :] = gro[0:3, width:]
    small[6:7, :] = jnp.broadcast_to(squared, (1, width))
    sm_cps = [
        send(small, smrecv_cx.at[group], gr_s.at[2, k], gr_r.at[2, k], c=flip(dc), x=lax.rem(x + dx, NX))
        for k, (dc, dx) in enumerate(cx_peers())
    ]
    smrecv_cx[group] = small[...]
    gown[...] = dot(jt[rows(384 * c, 384), :], dpre)
    qw = 2 * width // NX
    gx = {}
    for d in order:
        g_c[d].wait()
        gsum = gown[block(d), :] + gcr[block(d), :].astype(F32)
        gown[block(d), :] = gsum
        gxs[block(d), :] = gsum.astype(BF)
        gx[d] = [
            send(gxs.at[block(d), lanes(lax.rem(quarter + k, NX) * qw, qw)], gxr.at[k, block(d)],
                 gx_s.at[k, d], gx_r.at[k, d], **along(k))
            for k in range(1, NX)
        ]
    done(sm_cps)
    acc_s = sum_of(smrecv_cx, 8)
    smy[...] = acc_s
    smrecv_y[y] = acc_s
    sm_cps = [
        send(smy, smrecv_y.at[y], gr_s.at[4, d], gr_r.at[4, d], y=lax.rem(y + d, NY)) for d in range(1, NY)
    ]
    gz = []
    for d in order:
        done(gx[d])
        acc_g = gown[block(d), lanes(quarter * qw, qw)]
        for k in range(1, NX):
            acc_g += gxr[k, block(d), :].astype(F32)
        gzs[block(d), :] = acc_g.astype(BF)
        if d:
            gz.append((d, send(gzs.at[block(d)], gzr.at[d], gr_s.at[6, d], gr_r.at[6, d], z=lax.rem(z + d, NZ))))
    done(sm_cps)
    acc_s = sum_of(smrecv_y, NY)
    smz[...] = acc_s
    smrecv_z[z] = acc_s
    sm_cps = [
        send(smz, smrecv_z.at[z], gr_s.at[5, d], gr_r.at[5, d], z=lax.rem(z + d, NZ)) for d in range(1, NZ)
    ]
    for d, cp in gz:
        cp.wait()
        acc_g += gzr[d].astype(F32)
    gys[0] = acc_g.astype(BF)
    g_b = [send(gys.at[0], gyr.at[0, d], gr_s.at[7, d], gr_r.at[7, d], **across(d)) for d in range(1, NY)]
    done(sm_cps)
    acc_s = sum_of(smrecv_z, NZ)
    gro_out[:, 0:width] = acc_s[0:3]
    gro_out[:, width:] = acc_s[3:6]
    loss_out[...] = acc_s[6:7, 0:1] / (3.0 * rays_total)
    done(g_b)
    place = x * c + y * (1 - c)
    gfs[...] = ordered(gyr, gys, 0, place, NY)

    def final(k, row, slot, **where):
        return pltpu.make_async_remote_copy(
            src_ref=gfs.at[pl.ds(pl.multiple_of(row * 24, 8), 24)], dst_ref=gfr.at[slot],
            send_sem=gr_s.at[8, k], recv_sem=gr_r.at[8, slot],
            device_id=where, device_id_type=pl.DeviceIdType.MESH,
        )

    low_half = y // 2 == 0
    keeps = y // 2 == c
    own_row = lax.rem(y, 2)

    @pl.when(keeps)
    def _():
        gfr[quarter] = gfs[pl.ds(pl.multiple_of(own_row * 24, 8), 24), :]

    def to_x(act):
        for k, (dc, dx) in enumerate(cx_peers()):
            act(final(k, own_row, quarter, c=flip(dc), x=lax.rem(x + dx, NX)))

    def to_y(act):
        for k in range(4):
            yy, cc = 2 + k // 2, k % 2

            @pl.when(jnp.logical_not((y == yy) & (c == cc)))
            def _():
                act(final(k, k // 2, quarter, y=yy, c=cc))

    @pl.when((c == 0) & low_half)
    def _():
        to_x(lambda cp: cp.start())

    @pl.when(c == 1)
    def _():
        to_y(lambda cp: cp.start())

    for slot in range(NX):
        @pl.when(jnp.logical_not(keeps & (quarter == slot)))
        def _():
            final(0, 0, slot, c=1 - c).wait_recv()

        blk = gfr[slot]
        gin_out[:, qw * slot : qw * slot + qw] = jnp.where(c == 0, blk[0:12], blk[12:24])

    @pl.when((c == 0) & low_half)
    def _():
        to_x(lambda cp: cp.wait_send())

    @pl.when(c == 1)
    def _():
        to_y(lambda cp: cp.wait_send())


def sum_of(buf, n):
    acc = buf[0]
    for j in range(1, n):
        acc += buf[j]
    return acc


def ordered(recv, own, t, me, n):
    acc = None
    for j in range(n):
        d = lax.rem(me - j + n, n)
        val = jnp.where(d == 0, own[t].astype(F32), recv[t, d].astype(F32))
        acc = val if acc is None else acc + val
    return acc


def on_device(
    patches, patch_view, rays, ray_view, targets, camera, slots_init, key_weight, value_weight,
    query_weight, gru_input, gru_hidden, mix_query, mix_key, render_in, render_out,
):
    n, width = patches.shape
    V, S = pltpu.VMEM, pltpu.SemaphoreType.DMA
    vm = pl.BlockSpec(memory_space=pltpu.VMEM)
    scratch = (
        [V((128, L // NX), BF) for L in LEN]
        + [V((width, L), BF) for L in LEN]
        + [V((16, L), BF) for L in LEN]
        + [
            V((128, 24), F32), V((16, width), BF), V((128, width // 2), BF), V((512, width), BF),
            V((n, width), BF), V((n, width), F32), V((n, width), BF), V((8, 2 * width), BF), V((8, width), F32),
            V((3, 8, 8, width + 128), BF), V((3, 8, 8, width + 128), BF),
            V((3, 8, width + 128), BF), V((3, NY, 8, width + 128), BF),
            V((3, 8, width + 128), BF), V((3, NZ, 8, width + 128), BF),
            V((3, 8, width), BF), V((3, 8, 8, width), BF), V((8, width), F32), V((64, width), F32),
            V((8, n), F32), V((8, width), F32), V((8, 8, width), F32), V((NY, 8, width), F32), V((NZ, 8, width), F32),
            V((8, width), F32), V((8, width), F32),
            V((width, n), BF), V((384, 2 * width), F32), V((384, 2 * width), BF), V((384, 2 * width), BF),
            V((384, 2 * width), BF), V((NX, 384, width // 2), BF), V((384, width // 2), BF), V((NZ, 48, width // 2), BF),
            V((1, 48, width // 2), BF), V((1, NY, 48, width // 2), BF), V((48, width // 2), F32), V((NX, 24, width // 2), F32),
            S((5, 7)), S((5, 7)), S((5, 8)), S((5, 8)), S((5, 4, 8)), S((5, 4, 8)), S((5, 8)), S((5, 8)),
            S((3, 32)), S((3, 32)), S((9, 8)), S((9, 8)), S((8,)), S((8,)), S((4, 8)), S((4, 8)),
        ]
    )
    out = pl.pallas_call(
        kernel,
        out_shape=[
            jax.ShapeDtypeStruct((64, width), F32),
            jax.ShapeDtypeStruct((3, n), F32),
            jax.ShapeDtypeStruct((1, 1), F32),
            jax.ShapeDtypeStruct((12, 2 * width), F32),
            jax.ShapeDtypeStruct((3, 2 * width), F32),
        ],
        in_specs=[vm] * 16,
        out_specs=[vm] * 5,
        scratch_shapes=scratch,
        compiler_params=pltpu.CompilerParams(collective_id=0, has_side_effects=True, vmem_limit_bytes=60 << 20),
    )(
        patch_view[None], ray_view[None], patches, rays, targets, slots_init, camera, query_weight, key_weight,
        value_weight, mix_key, gru_input, gru_hidden, mix_query, render_in, render_out,
    )
    slots, colour, loss, gin, gro = out
    return slots, colour, loss[0, 0], gin, gro


def solution(mesh):
    torus = Mesh(mesh.devices.reshape(NZ, NY, NC, NX), ("z", "y", "c", "x"))
    tok, every = ("z", "y", "c"), ("z", "y", "c", "x")
    w = P(tok, None)
    return jax.shard_map(
        on_device,
        mesh=torus,
        in_specs=(
            P(every, None), P(every), P(every, None), P(every), P(None, every), w, P(),
            w, w, w, w, w, w, w, w, P(None, tok),
        ),
        out_specs=(P(), P(None, every), P(), w, P()),
        check_vma=False,
    )
```

```python
import functools

import jax
import jax.numpy as jnp
from jax import lax
from jax.experimental import pallas as pl
from jax.experimental.pallas import tpu as pltpu
from jax.sharding import Mesh
from jax.sharding import PartitionSpec as P

ITERS = 3
EPSILON = 1e-05
ATTN_FLOOR = 1e-08
NZ, NY, NC, NX = 8, 4, 2, 4
BF = jnp.bfloat16
F32 = jnp.float32

LEN = (1536, 1536, 4608, 2560)
NB = 4


def dot(a, b, ca=1, cb=0):
    return lax.dot_general(a, b, (((ca,), (cb,)), ((), ())), preferred_element_type=F32)


def normalize(values):
    mean = jnp.mean(values, axis=-1, keepdims=True)
    centred = values - mean
    spread = jnp.mean(centred * centred, axis=-1, keepdims=True)
    return centred * lax.rsqrt(spread + EPSILON)


def onehot(mask):
    return mask.astype(F32).astype(BF)


def softmax0(logits):
    top = jnp.max(logits, axis=0, keepdims=True)
    e = jnp.exp(logits - top)
    return e / jnp.sum(e, axis=0, keepdims=True)


def rows(start, size):
    return pl.ds(pl.multiple_of(start, 16), size)


def lanes(start, size):
    return pl.ds(pl.multiple_of(start, 128), size)


def kernel(
    pview, rview, patches, rays, targets, slots_init, camera,
    wq, wk, wv, mk, gi, gh, mq, rin_w, rout,
    slots_out, colour_out, loss_out, gin_out, gro_out,
    cy0, cy1, cy2, cy3, f0, f1, f2, f3, sg0, sg1, sg2, sg3, rp, camsg, camcy, camf,
    px, rin, rx, ro, state, tsend, trecv, tysend, tyrecv, tzsend, tzrecv,
    psend, precv, ssend, srecv, dcol8, small, smrecv_cx, smrecv_y, smrecv_z, smy, smz,
    jt, gown, gcs, gcr, gxs, gxr, gzs, gzr, gys, gyr, gfs, gfr,
    cy_s, cy_r, z_s, z_r, x_s, x_r, c_s, c_r, it_s, it_r, gr_s, gr_r, gc_s, gc_r, gx_s, gx_r,
):
    z, y, c, x = (lax.axis_index(a) for a in ("z", "y", "c", "x"))
    cyb, full, stage = (cy0, cy1, cy2, cy3), (f0, f1, f2, f3), (sg0, sg1, sg2, sg3)
    width = patches.shape[1]
    scale = width ** (-0.5)
    pending = []

    def send(src, dst, ssem, rsem, **where):
        cp = pltpu.make_async_remote_copy(
            src_ref=src, dst_ref=dst, send_sem=ssem, recv_sem=rsem,
            device_id=where, device_id_type=pl.DeviceIdType.MESH,
        )
        cp.start()
        pending.append(cp)
        return cp

    def yc_peers():
        return [(dy, dc) for dy in range(NY) for dc in range(NC) if dy or dc]

    def cx_peers():
        return [(dc, dx) for dc in range(NC) for dx in range(NX) if dc or dx]

    def flip(dc):
        return 1 - c if dc else c

    barrier = pltpu.get_barrier_semaphore()
    met = 0
    for dy, dc in yc_peers():
        pl.semaphore_signal(barrier, inc=1, device_id={"y": lax.rem(y + dy, NY), "c": flip(dc)}, device_id_type=pl.DeviceIdType.MESH)
        met += 1
    for dc, dx in cx_peers():
        if dx:
            pl.semaphore_signal(barrier, inc=1, device_id={"x": lax.rem(x + dx, NX), "c": flip(dc)}, device_id_type=pl.DeviceIdType.MESH)
            met += 1
    for dz in range(1, NZ):
        pl.semaphore_signal(barrier, inc=1, device_id={"z": lax.rem(z + dz, NZ)}, device_id_type=pl.DeviceIdType.MESH)
        met += 1
    pl.semaphore_wait(barrier, met)

    me_yc = y * 2 + c
    quarter = x * (1 - c) + y * c

    def along(d):
        return dict(x=lax.rem(x + d * (1 - c), NX), y=lax.rem(y + d * c, NY))

    def across(d):
        return dict(x=lax.rem(x + d * c, NX), y=lax.rem(y + d * (1 - c), NY))

    def yc_copies(src, buf, slot, w, part):
        out = []
        for k, (dy, dc) in enumerate(yc_peers()):
            yy, cc = lax.rem(y + dy, NY), flip(dc)
            cp = pltpu.make_async_remote_copy(
                src_ref=src.at[:, lanes(part(yy, cc) * w, w)], dst_ref=buf.at[rows(me_yc * 16, 16)],
                send_sem=cy_s.at[slot, k], recv_sem=cy_r.at[slot, k],
                device_id={"y": yy, "c": cc}, device_id_type=pl.DeviceIdType.MESH,
            )
            out.append((cp, dy, cc))
        return out

    def pack(b, parts):
        stage[b][...] = jnp.zeros_like(stage[b])
        at = 0
        for part in parts:
            stage[b][0:12, at : at + part.shape[1]] = part[...]
            at += part.shape[1]

    def pack_colour(at):
        rp[...] = jnp.zeros_like(rp)
        rp[0:3, :] = rout[...].astype(F32)
        unit = lax.broadcasted_iota(jnp.int32, (16, 24), 1)
        row = lax.broadcasted_iota(jnp.int32, (16, 24), 0)
        for j in range(2):
            mask = (unit == row + 12 * j) & (row < 12)
            stage[3][:, at + 128 * j : at + 128 * j + 128] = dot(onehot(mask), rp[...].astype(BF), 1, 1).astype(BF)

    def start_bundle(b):
        w = LEN[b] // NX
        cyb[b][rows(me_yc * 16, 16), :] = stage[b][:, lanes(quarter * w, w)]
        cps = yc_copies(stage[b], cyb[b], b, w, lambda yy, cc: x * (1 - cc) + yy * cc)
        for cp, dy, cc in cps:
            @pl.when(y // 2 == cc)
            def _():
                cp.start()

        return cps

    def finish_bundle(cps):
        for cp, dy, cc in cps:
            @pl.when(lax.rem(y - dy + NY, NY) // 2 == c)
            def _():
                cp.wait_recv()

            @pl.when(y // 2 == cc)
            def _():
                cp.wait_send()

    def compact(shards, real, first, count):
        n = shards.shape[0]
        r = lax.broadcasted_iota(jnp.int32, (count, n), 0) + first
        k = lax.broadcasted_iota(jnp.int32, (count, n), 1)
        lane = k % 16
        mask = (lane < real) & (r == (k // 16) * real + lane)
        return dot(onehot(mask), shards).astype(BF)

    def piece(b, zz):
        w = LEN[b] // NX
        return full[b].at[rows(zz * 96 + c * 48, 48), lanes(quarter * w, w)]

    def start_z(b, arrived, ring=True):
        finish_bundle(arrived)
        w = LEN[b] // NX
        full[b][rows(z * 96 + c * 48, 48), lanes(quarter * w, w)] = compact(cyb[b][rows(c * 64, 64), :], 12, 0, 48)
        if not ring:
            return [
                send(piece(b, z), piece(b, z), z_s.at[b, d], z_r.at[b, d], z=lax.rem(z + d, NZ))
                for d in range(1, NZ)
            ]
        return [pass_on(b, z, 1), pass_on(b, z, NZ - 1)]

    def pass_on(b, zz, d):
        to = lax.rem(z + (1 if d <= NZ // 2 else NZ - 1), NZ)
        return send(piece(b, zz), piece(b, zz), z_s.at[b, d], z_r.at[b, d], z=to)

    def forward_x(b, ref, d):
        return [send(ref, ref, x_s.at[b, k, d], x_r.at[b, k, d], **along(k)) for k in range(1, NX)]

    out, sent = {}, {}

    def ring_steps(bundles):
        for b, first in bundles:
            out[b] = [(0, forward_x(b, piece(b, z), 0))]
            sent[b] = list(first)
        yield
        for k in range(1, NZ // 2 + 1):
            for d in (k, NZ - k) if k < NZ // 2 else (k,):
                for b, _ in bundles:
                    zz = lax.rem(z - d + NZ, NZ)
                    pltpu.make_async_remote_copy(
                        src_ref=piece(b, zz), dst_ref=piece(b, zz), send_sem=z_s.at[b, d], recv_sem=z_r.at[b, d],
                        device_id={"z": zz}, device_id_type=pl.DeviceIdType.MESH,
                    ).wait_recv()
                    if d < NZ // 2:
                        sent[b].append(pass_on(b, zz, d + 1))
                    if d > NZ // 2 + 1:
                        sent[b].append(pass_on(b, zz, d - 1))
                    out[b].append((d, forward_x(b, piece(b, zz), d)))
            yield

    def swap_core(b, gathered):
        arriving, sent = gathered
        for cp in sent:
            cp.wait_send()
        cps = []
        for d, group_cps in arriving:
            for cp in group_cps:
                cp.wait()
            ref = full[b].at[rows(lax.rem(z - d + NZ, NZ) * 96 + c * 48, 48)]
            cps.append(send(ref, ref, c_s.at[b, d], c_r.at[b, d], c=1 - c))
        return cps

    def done(cps):
        for cp in cps:
            cp.wait()

    half = width // 2
    pack(0, (wq, wk))
    cy_b0 = start_bundle(0)
    camsg[...] = jnp.zeros_like(camsg)
    camsg[0:8, :] = camera[...]
    camcy[rows(me_yc * 16, 16), :] = camsg[:, lanes(c * half, half)]
    cy_cam = yc_copies(camsg, camcy, 4, half, lambda yy, cc: cc)
    for cp, _, _ in cy_cam:
        cp.start()
    n0 = normalize(slots_init[...]).astype(BF)
    z_b0 = start_z(0, cy_b0)
    for cp, _, _ in cy_cam:
        cp.wait()
    camf[rows(z * 64 + quarter * 16, 16), lanes(c * half, half)] = compact(camcy[...], 8, quarter * 16, 16)

    def cam_piece(zz):
        return camf.at[rows(zz * 64 + quarter * 16, 16), lanes(c * half, half)]

    z_cam = [
        send(cam_piece(z), cam_piece(z), z_s.at[4, d], z_r.at[4, d], z=lax.rem(z + d, NZ))
        for d in range(1, NZ)
    ]
    pack(1, (wv, mk))
    cy_b1 = start_bundle(1)
    pack(2, (gi, gh))
    cy_b2 = start_bundle(2)
    for _ in ring_steps([(0, z_b0)]):
        pass
    z_b1 = start_z(1, cy_b1)
    z_b2 = start_z(2, cy_b2)
    x_cam = forward_x(4, cam_piece(z), 0)
    for d in range(1, NZ):
        z_cam[d - 1].wait()
        x_cam += forward_x(4, cam_piece(lax.rem(z - d + NZ, NZ)), d)
    ring = ring_steps([(1, z_b1), (2, z_b2)])
    next(ring)
    c_b0 = swap_core(0, (out[0], sent[0]))
    next(ring)
    done(x_cam)
    cam_half = camf.at[:, lanes(c * half, half)]
    done([send(cam_half, cam_half, c_s.at[4, 0], c_r.at[4, 0], c=1 - c)])

    def lookup(view):
        v = lax.broadcasted_iota(jnp.int32, (camf.shape[0], view.shape[1]), 0)
        return dot(onehot(v == view[...]), camf[...], 0, 0)

    px[...] = normalize(patches[...].astype(F32) + lookup(pview)).astype(BF)
    next(ring)
    pack(3, (mq, rin_w))
    pack_colour(3 * width)
    cy_b3 = start_bundle(3)
    done(c_b0)

    def slot_projection(normed):
        query = (dot(normed, f0[:, 0:width]) * scale).astype(BF)
        return dot(query, f0[:, width : 2 * width], 1, 1).astype(BF)

    group = c * NX + x
    mine = pl.ds(pl.multiple_of(group * 8, 8), 8)
    state[...] = slots_init[mine, :]
    proj = slot_projection(n0)
    x_b3, c_b3 = [], []
    gaps = ((0, 1, 2, 3), (4, 5, 6, 7), ())

    def group_rows(buf, t):
        return jnp.concatenate([buf[t, g].astype(F32) for g in range(8)], axis=0)

    def share(t, value):
        psend[t] = value
        precv[t, group] = value
        return [
            send(psend.at[t], precv.at[t, group], it_s.at[t, 24 + k], it_r.at[t, 24 + k],
                 c=flip(dc), x=lax.rem(x + dx, NX))
            for k, (dc, dx) in enumerate(cx_peers())
        ]

    for t in range(ITERS):
        attn = softmax0(dot(proj, px[...], 1, 1)) + ATTN_FLOOR
        total = dot(attn.astype(BF), px[...])
        denom = jnp.sum(attn, axis=1, keepdims=True)
        for g in range(8):
            tsend[t, g, :, 0:width] = total[8 * g : 8 * g + 8].astype(BF)
            tsend[t, g, :, width : width + 128] = jnp.broadcast_to(denom[8 * g : 8 * g + 8], (8, 128)).astype(BF)
        cps = []
        for k, (dc, dx) in enumerate(cx_peers()):
            cc, xx = flip(dc), lax.rem(x + dx, NX)
            cps.append(send(tsend.at[t, cc * NX + xx], trecv.at[t, k], it_s.at[t, k], it_r.at[t, k], c=cc, x=xx))
        if t == 0:
            for _ in ring:
                pass
            z_b3 = start_z(3, cy_b3, ring=False)
        acc = tsend[t, group].astype(F32)
        for k, cp in enumerate(cps):
            cp.wait()
            acc += trecv[t, k].astype(F32)
        tysend[t] = acc.astype(BF)
        cps = [
            send(tysend.at[t], tyrecv.at[t, d], it_s.at[t, 8 + d], it_r.at[t, 8 + d], y=lax.rem(y + d, NY))
            for d in range(1, NY)
        ]
        for cp in cps:
            cp.wait()
        acc = ordered(tyrecv, tysend, t, y, NY)
        tzsend[t] = acc.astype(BF)
        cps = [
            send(tzsend.at[t], tzrecv.at[t, d], it_s.at[t, 12 + d], it_r.at[t, 12 + d], z=lax.rem(z + d, NZ))
            for d in range(1, NZ)
        ]
        if t == 0:
            c_b1 = swap_core(1, (out[1], sent[1]))
            c_b2 = swap_core(2, (out[2], sent[2]))
        if t:
            c_b3 += swap_core(3, (x_b3, []))
            x_b3 = []
        for d in gaps[t]:
            if d:
                z_b3[d - 1].wait()
            x_b3.append((d, forward_x(3, piece(3, lax.rem(z - d + NZ, NZ)), d)))
        if t == 1:
            rin[...] = rays[...].astype(F32) + lookup(rview)
            rx[...] = rin[...].astype(BF)
        if t == 2:
            done(c_b3)
            r = lax.broadcasted_iota(jnp.int32, (width, 1), 0)
            hid = 2 * r - r % 12
            unit = lax.broadcasted_iota(jnp.int32, (width, 2 * width), 1)
            ro[...] = (
                dot(f3[:, 3 * width : 3 * width + 128], onehot(unit == hid), 0, 0)
                + dot(f3[:, 3 * width + 128 : 3 * width + 256], onehot(unit == hid + 12), 0, 0)
            )[0:8].astype(BF)
        for cp in cps:
            cp.wait()
        acc = ordered(tzrecv, tzsend, t, z, NZ)
        if t == 0:
            done(c_b1)
            done(c_b2)
        mean_x = (acc[:, 0:width] / acc[:, width : width + 1]).astype(BF)
        update = dot(mean_x, f1[:, 0:width]).astype(BF)
        slots = state[...]
        a = dot(update, f2[:, 0 : 3 * width])
        b = dot(slots.astype(BF), f2[:, 3 * width : 6 * width])
        reset = jax.nn.sigmoid(a[:, 0:width] + b[:, 0:width])
        blend = jax.nn.sigmoid(a[:, width : 2 * width] + b[:, width : 2 * width])
        cand = jnp.tanh(a[:, 2 * width :] + reset * b[:, 2 * width :])
        slots = (1.0 - blend) * cand + blend * slots
        state[...] = slots
        if t + 1 < ITERS:
            cps = share(t, slot_projection(normalize(slots).astype(BF)))
            done(cps)
            proj = group_rows(precv, t).astype(BF)

    t = ITERS - 1
    ssend[...] = slots
    srecv[mine, :] = slots
    s_cps = [
        send(ssend, srecv.at[mine], gr_s.at[0, k], gr_r.at[0, k], c=flip(dc), x=lax.rem(x + dx, NX))
        for k, (dc, dx) in enumerate(cx_peers())
    ]
    slot_keys = dot(slots.astype(BF), f1[:, width : 2 * width]).astype(BF)
    r_cps = share(t, (dot(slot_keys, f3[:, 0:width], 1, 1) * scale).astype(BF))
    done(s_cps)
    done(r_cps)
    slots_all = srecv[...]
    slots_out[...] = slots_all
    low = slots_all.astype(BF)
    mix = softmax0(dot(group_rows(precv, t).astype(BF), rx[...], 1, 1)).astype(BF)
    joined = (dot(mix, low, 0, 0) + rin[...]).astype(BF)
    pre = dot(joined, f3[:, width : 3 * width])
    sig = jax.nn.sigmoid(pre)
    hidden = (pre * sig).astype(BF)
    colour = dot(ro[...], hidden, 1, 1)[0:3]
    colour_out[...] = colour
    error = colour - targets[...]
    rays_total = rin.shape[0] * NZ * NY * NC * NX
    dcol8[...] = jnp.zeros_like(dcol8)
    dcol8[0:3, :] = error * (2.0 / jnp.sqrt(jnp.float32(3.0 * rays_total)))
    dcol = dcol8[...].astype(BF)
    dpre = (dot(dcol, ro[...], 0, 0) * (sig + pre * sig * (1.0 - sig))).astype(BF)
    gro = dot(dcol, hidden)
    squared = jnp.sum(jnp.sum(error * error, axis=1, keepdims=True), axis=0, keepdims=True)

    turned = jnp.transpose(joined.astype(F32)).astype(BF)
    for zz in range(NZ):
        for h in range(NC):
            jt[384 * h + 48 * zz : 384 * h + 48 * zz + 48, :] = turned[96 * zz + 48 * h : 96 * zz + 48 * h + 48]
    order = (4, 3, 5, 2, 6, 1, 7, 0)

    def block(d):
        return rows(lax.rem(z + d, NZ) * 48, 48)

    gcs[...] = dot(jt[rows(384 * (1 - c), 384), :], dpre).astype(BF)
    g_c = {d: send(gcs.at[block(d)], gcr.at[block(d)], gc_s.at[d], gc_r.at[d], c=1 - c) for d in order}
    small[...] = jnp.zeros_like(small)
    small[0:3, :] = gro[0:3, 0:width]
    small[3:6, :] = gro[0:3, width:]
    small[6:7, :] = jnp.broadcast_to(squared, (1, width))
    sm_cps = [
        send(small, smrecv_cx.at[group], gr_s.at[2, k], gr_r.at[2, k], c=flip(dc), x=lax.rem(x + dx, NX))
        for k, (dc, dx) in enumerate(cx_peers())
    ]
    smrecv_cx[group] = small[...]
    gown[...] = dot(jt[rows(384 * c, 384), :], dpre)
    qw = 2 * width // NX
    gx = {}
    for d in order:
        g_c[d].wait()
        gsum = gown[block(d), :] + gcr[block(d), :].astype(F32)
        gown[block(d), :] = gsum
        gxs[block(d), :] = gsum.astype(BF)
        gx[d] = [
            send(gxs.at[block(d), lanes(lax.rem(quarter + k, NX) * qw, qw)], gxr.at[k, block(d)],
                 gx_s.at[k, d], gx_r.at[k, d], **along(k))
            for k in range(1, NX)
        ]
    done(sm_cps)
    acc_s = sum_of(smrecv_cx, 8)
    smy[...] = acc_s
    smrecv_y[y] = acc_s
    sm_cps = [
        send(smy, smrecv_y.at[y], gr_s.at[4, d], gr_r.at[4, d], y=lax.rem(y + d, NY)) for d in range(1, NY)
    ]
    gz = []
    for d in order:
        done(gx[d])
        acc_g = gown[block(d), lanes(quarter * qw, qw)]
        for k in range(1, NX):
            acc_g += gxr[k, block(d), :].astype(F32)
        gzs[block(d), :] = acc_g.astype(BF)
        if d:
            gz.append((d, send(gzs.at[block(d)], gzr.at[d], gr_s.at[6, d], gr_r.at[6, d], z=lax.rem(z + d, NZ))))
    done(sm_cps)
    acc_s = sum_of(smrecv_y, NY)
    smz[...] = acc_s
    smrecv_z[z] = acc_s
    sm_cps = [
        send(smz, smrecv_z.at[z], gr_s.at[5, d], gr_r.at[5, d], z=lax.rem(z + d, NZ)) for d in range(1, NZ)
    ]
    for d, cp in gz:
        cp.wait()
        acc_g += gzr[d].astype(F32)
    gys[0] = acc_g.astype(BF)
    g_b = [send(gys.at[0], gyr.at[0, d], gr_s.at[7, d], gr_r.at[7, d], **across(d)) for d in range(1, NY)]
    done(sm_cps)
    acc_s = sum_of(smrecv_z, NZ)
    gro_out[:, 0:width] = acc_s[0:3]
    gro_out[:, width:] = acc_s[3:6]
    loss_out[...] = acc_s[6:7, 0:1] / (3.0 * rays_total)
    done(g_b)
    place = x * c + y * (1 - c)
    gfs[...] = ordered(gyr, gys, 0, place, NY)

    def final(k, row, slot, **where):
        return pltpu.make_async_remote_copy(
            src_ref=gfs.at[pl.ds(pl.multiple_of(row * 24, 8), 24)], dst_ref=gfr.at[slot],
            send_sem=gr_s.at[8, k], recv_sem=gr_r.at[8, slot],
            device_id=where, device_id_type=pl.DeviceIdType.MESH,
        )

    low_half = y // 2 == 0
    keeps = y // 2 == c
    own_row = lax.rem(y, 2)

    @pl.when(keeps)
    def _():
        gfr[quarter] = gfs[pl.ds(pl.multiple_of(own_row * 24, 8), 24), :]

    def to_x(act):
        for k, (dc, dx) in enumerate(cx_peers()):
            act(final(k, own_row, quarter, c=flip(dc), x=lax.rem(x + dx, NX)))

    def to_y(act):
        for k in range(4):
            yy, cc = 2 + k // 2, k % 2

            @pl.when(jnp.logical_not((y == yy) & (c == cc)))
            def _():
                act(final(k, k // 2, quarter, y=yy, c=cc))

    @pl.when((c == 0) & low_half)
    def _():
        to_x(lambda cp: cp.start())

    @pl.when(c == 1)
    def _():
        to_y(lambda cp: cp.start())

    for slot in range(NX):
        @pl.when(jnp.logical_not(keeps & (quarter == slot)))
        def _():
            final(0, 0, slot, c=1 - c).wait_recv()

        blk = gfr[slot]
        gin_out[:, qw * slot : qw * slot + qw] = jnp.where(c == 0, blk[0:12], blk[12:24])

    @pl.when((c == 0) & low_half)
    def _():
        to_x(lambda cp: cp.wait_send())

    @pl.when(c == 1)
    def _():
        to_y(lambda cp: cp.wait_send())


def sum_of(buf, n):
    acc = buf[0]
    for j in range(1, n):
        acc += buf[j]
    return acc


def ordered(recv, own, t, me, n):
    acc = None
    for j in range(n):
        d = lax.rem(me - j + n, n)
        val = jnp.where(d == 0, own[t].astype(F32), recv[t, d].astype(F32))
        acc = val if acc is None else acc + val
    return acc


def on_device(
    patches, patch_view, rays, ray_view, targets, camera, slots_init, key_weight, value_weight,
    query_weight, gru_input, gru_hidden, mix_query, mix_key, render_in, render_out,
):
    n, width = patches.shape
    V, S = pltpu.VMEM, pltpu.SemaphoreType.DMA
    vm = pl.BlockSpec(memory_space=pltpu.VMEM)
    scratch = (
        [V((128, L // NX), BF) for L in LEN]
        + [V((width, L), BF) for L in LEN]
        + [V((16, L), BF) for L in LEN]
        + [
            V((128, 24), F32), V((16, width), BF), V((128, width // 2), BF), V((512, width), BF),
            V((n, width), BF), V((n, width), F32), V((n, width), BF), V((8, 2 * width), BF), V((8, width), F32),
            V((3, 8, 8, width + 128), BF), V((3, 8, 8, width + 128), BF),
            V((3, 8, width + 128), BF), V((3, NY, 8, width + 128), BF),
            V((3, 8, width + 128), BF), V((3, NZ, 8, width + 128), BF),
            V((3, 8, width), BF), V((3, 8, 8, width), BF), V((8, width), F32), V((64, width), F32),
            V((8, n), F32), V((8, width), F32), V((8, 8, width), F32), V((NY, 8, width), F32), V((NZ, 8, width), F32),
            V((8, width), F32), V((8, width), F32),
            V((width, n), BF), V((384, 2 * width), F32), V((384, 2 * width), BF), V((384, 2 * width), BF),
            V((384, 2 * width), BF), V((NX, 384, width // 2), BF), V((384, width // 2), BF), V((NZ, 48, width // 2), BF),
            V((1, 48, width // 2), BF), V((1, NY, 48, width // 2), BF), V((48, width // 2), F32), V((NX, 24, width // 2), F32),
            S((5, 7)), S((5, 7)), S((5, 8)), S((5, 8)), S((5, 4, 8)), S((5, 4, 8)), S((5, 8)), S((5, 8)),
            S((3, 32)), S((3, 32)), S((9, 8)), S((9, 8)), S((8,)), S((8,)), S((4, 8)), S((4, 8)),
        ]
    )
    out = pl.pallas_call(
        kernel,
        out_shape=[
            jax.ShapeDtypeStruct((64, width), F32),
            jax.ShapeDtypeStruct((3, n), F32),
            jax.ShapeDtypeStruct((1, 1), F32),
            jax.ShapeDtypeStruct((12, 2 * width), F32),
            jax.ShapeDtypeStruct((3, 2 * width), F32),
        ],
        in_specs=[vm] * 16,
        out_specs=[vm] * 5,
        scratch_shapes=scratch,
        compiler_params=pltpu.CompilerParams(collective_id=0, has_side_effects=True, vmem_limit_bytes=60 << 20),
    )(
        patch_view[None], ray_view[None], patches, rays, targets, slots_init, camera, query_weight, key_weight,
        value_weight, mix_key, gru_input, gru_hidden, mix_query, render_in, render_out,
    )
    slots, colour, loss, gin, gro = out
    return slots, colour, loss[0, 0], gin, gro


def solution(mesh):
    torus = Mesh(mesh.devices.reshape(NZ, NY, NC, NX), ("z", "y", "c", "x"))
    tok, every = ("z", "y", "c"), ("z", "y", "c", "x")
    w = P(tok, None)
    return jax.shard_map(
        on_device,
        mesh=torus,
        in_specs=(
            P(every, None), P(every), P(every, None), P(every), P(None, every), w, P(),
            w, w, w, w, w, w, w, w, P(None, tok),
        ),
        out_specs=(P(), P(None, every), P(), w, P()),
        check_vma=False,
    )
```

```python
import functools

import jax
import jax.numpy as jnp
from jax import lax
from jax.experimental import pallas as pl
from jax.experimental.pallas import tpu as pltpu
from jax.sharding import Mesh
from jax.sharding import PartitionSpec as P

ITERS = 3
EPSILON = 1e-05
ATTN_FLOOR = 1e-08
NZ, NY, NC, NX = 8, 4, 2, 4
BF = jnp.bfloat16
F32 = jnp.float32

LEN = (1536, 1536, 4608, 2560)
NB = 4


def dot(a, b, ca=1, cb=0):
    return lax.dot_general(a, b, (((ca,), (cb,)), ((), ())), preferred_element_type=F32)


def normalize(values):
    mean = jnp.mean(values, axis=-1, keepdims=True)
    centred = values - mean
    spread = jnp.mean(centred * centred, axis=-1, keepdims=True)
    return centred * lax.rsqrt(spread + EPSILON)


def onehot(mask):
    return mask.astype(F32).astype(BF)


def softmax0(logits):
    top = jnp.max(logits, axis=0, keepdims=True)
    e = jnp.exp(logits - top)
    return e / jnp.sum(e, axis=0, keepdims=True)


def rows(start, size):
    return pl.ds(pl.multiple_of(start, 16), size)


def lanes(start, size):
    return pl.ds(pl.multiple_of(start, 128), size)


def kernel(
    pview, rview, patches, rays, targets, slots_init, camera,
    wq, wk, wv, mk, gi, gh, mq, rin_w, rout,
    slots_out, colour_out, loss_out, gin_out, gro_out,
    cy0, cy1, cy2, cy3, f0, f1, f2, f3, sg0, sg1, sg2, sg3, rp, camsg, camcy, camf,
    px, rin, rx, ro, state, tsend, trecv, tysend, tyrecv, tzsend, tzrecv,
    psend, precv, ssend, srecv, dcol8, small, smrecv_cx, smrecv_y, smrecv_z, smy, smz,
    jt, gown, gcs, gcr, gxs, gxr, gzs, gzr, gys, gyr, gfs, gfr,
    cy_s, cy_r, z_s, z_r, x_s, x_r, c_s, c_r, it_s, it_r, gr_s, gr_r, gc_s, gc_r, gx_s, gx_r,
):
    z, y, c, x = (lax.axis_index(a) for a in ("z", "y", "c", "x"))
    cyb, full, stage = (cy0, cy1, cy2, cy3), (f0, f1, f2, f3), (sg0, sg1, sg2, sg3)
    width = patches.shape[1]
    scale = width ** (-0.5)
    pending = []

    def send(src, dst, ssem, rsem, **where):
        cp = pltpu.make_async_remote_copy(
            src_ref=src, dst_ref=dst, send_sem=ssem, recv_sem=rsem,
            device_id=where, device_id_type=pl.DeviceIdType.MESH,
        )
        cp.start()
        pending.append(cp)
        return cp

    def yc_peers():
        return [(dy, dc) for dy in range(NY) for dc in range(NC) if dy or dc]

    def cx_peers():
        return [(dc, dx) for dc in range(NC) for dx in range(NX) if dc or dx]

    def flip(dc):
        return 1 - c if dc else c

    barrier = pltpu.get_barrier_semaphore()
    met = 0
    for dy, dc in yc_peers():
        pl.semaphore_signal(barrier, inc=1, device_id={"y": lax.rem(y + dy, NY), "c": flip(dc)}, device_id_type=pl.DeviceIdType.MESH)
        met += 1
    for dc, dx in cx_peers():
        if dx:
            pl.semaphore_signal(barrier, inc=1, device_id={"x": lax.rem(x + dx, NX), "c": flip(dc)}, device_id_type=pl.DeviceIdType.MESH)
            met += 1
    for dz in range(1, NZ):
        pl.semaphore_signal(barrier, inc=1, device_id={"z": lax.rem(z + dz, NZ)}, device_id_type=pl.DeviceIdType.MESH)
        met += 1

    me_yc = y * 2 + c
    quarter = x * (1 - c) + y * c

    def along(d):
        return dict(x=lax.rem(x + d * (1 - c), NX), y=lax.rem(y + d * c, NY))

    def across(d):
        return dict(x=lax.rem(x + d * c, NX), y=lax.rem(y + d * (1 - c), NY))

    def yc_copies(src, buf, slot, w, part):
        out = []
        for k, (dy, dc) in enumerate(yc_peers()):
            yy, cc = lax.rem(y + dy, NY), flip(dc)
            cp = pltpu.make_async_remote_copy(
                src_ref=src.at[:, lanes(part(yy, cc) * w, w)], dst_ref=buf.at[rows(me_yc * 16, 16)],
                send_sem=cy_s.at[slot, k], recv_sem=cy_r.at[slot, k],
                device_id={"y": yy, "c": cc}, device_id_type=pl.DeviceIdType.MESH,
            )
            out.append((cp, dy, cc))
        return out

    def pack(b, parts):
        stage[b][...] = jnp.zeros_like(stage[b])
        at = 0
        for part in parts:
            stage[b][0:12, at : at + part.shape[1]] = part[...]
            at += part.shape[1]

    def pack_colour(at):
        rp[...] = jnp.zeros_like(rp)
        rp[0:3, :] = rout[...].astype(F32)
        unit = lax.broadcasted_iota(jnp.int32, (16, 24), 1)
        row = lax.broadcasted_iota(jnp.int32, (16, 24), 0)
        for j in range(2):
            mask = (unit == row + 12 * j) & (row < 12)
            stage[3][:, at + 128 * j : at + 128 * j + 128] = dot(onehot(mask), rp[...].astype(BF), 1, 1).astype(BF)

    def start_bundle(b):
        w = LEN[b] // NX
        cyb[b][rows(me_yc * 16, 16), :] = stage[b][:, lanes(quarter * w, w)]
        cps = yc_copies(stage[b], cyb[b], b, w, lambda yy, cc: x * (1 - cc) + yy * cc)
        for cp, dy, cc in cps:
            @pl.when(y // 2 == cc)
            def _():
                cp.start()

        return cps

    def finish_bundle(cps):
        for cp, dy, cc in cps:
            @pl.when(lax.rem(y - dy + NY, NY) // 2 == c)
            def _():
                cp.wait_recv()

            @pl.when(y // 2 == cc)
            def _():
                cp.wait_send()

    def compact(shards, real, first, count):
        n = shards.shape[0]
        r = lax.broadcasted_iota(jnp.int32, (count, n), 0) + first
        k = lax.broadcasted_iota(jnp.int32, (count, n), 1)
        lane = k % 16
        mask = (lane < real) & (r == (k // 16) * real + lane)
        return dot(onehot(mask), shards).astype(BF)

    def piece(b, zz):
        w = LEN[b] // NX
        return full[b].at[rows(zz * 96 + c * 48, 48), lanes(quarter * w, w)]

    def start_z(b, arrived, ring=True):
        finish_bundle(arrived)
        w = LEN[b] // NX
        full[b][rows(z * 96 + c * 48, 48), lanes(quarter * w, w)] = compact(cyb[b][rows(c * 64, 64), :], 12, 0, 48)
        if not ring:
            return [
                send(piece(b, z), piece(b, z), z_s.at[b, d], z_r.at[b, d], z=lax.rem(z + d, NZ))
                for d in range(1, NZ)
            ]
        return [pass_on(b, z, 1), pass_on(b, z, NZ - 1)]

    def pass_on(b, zz, d):
        to = lax.rem(z + (1 if d <= NZ // 2 else NZ - 1), NZ)
        return send(piece(b, zz), piece(b, zz), z_s.at[b, d], z_r.at[b, d], z=to)

    def forward_x(b, ref, d):
        return [send(ref, ref, x_s.at[b, k, d], x_r.at[b, k, d], **along(k)) for k in range(1, NX)]

    out, sent = {}, {}

    def ring_steps(bundles):
        for b, first in bundles:
            out[b] = [(0, forward_x(b, piece(b, z), 0))]
            sent[b] = list(first)
        yield
        for k in range(1, NZ // 2 + 1):
            for d in (k, NZ - k) if k < NZ // 2 else (k,):
                for b, _ in bundles:
                    zz = lax.rem(z - d + NZ, NZ)
                    pltpu.make_async_remote_copy(
                        src_ref=piece(b, zz), dst_ref=piece(b, zz), send_sem=z_s.at[b, d], recv_sem=z_r.at[b, d],
                        device_id={"z": zz}, device_id_type=pl.DeviceIdType.MESH,
                    ).wait_recv()
                    if d < NZ // 2:
                        sent[b].append(pass_on(b, zz, d + 1))
                    if d > NZ // 2 + 1:
                        sent[b].append(pass_on(b, zz, d - 1))
                    out[b].append((d, forward_x(b, piece(b, zz), d)))
            yield

    def swap_core(b, gathered):
        arriving, sent = gathered
        for cp in sent:
            cp.wait_send()
        cps = []
        for d, group_cps in arriving:
            for cp in group_cps:
                cp.wait()
            ref = full[b].at[rows(lax.rem(z - d + NZ, NZ) * 96 + c * 48, 48)]
            cps.append(send(ref, ref, c_s.at[b, d], c_r.at[b, d], c=1 - c))
        return cps

    def done(cps):
        for cp in cps:
            cp.wait()

    half = width // 2
    pack(0, (wq, wk))
    pack(1, (wv, mk))
    pack(2, (gi, gh))
    pack(3, (mq, rin_w))
    pack_colour(3 * width)
    camsg[...] = jnp.zeros_like(camsg)
    camsg[0:8, :] = camera[...]
    pl.semaphore_wait(barrier, met)
    cy_b0 = start_bundle(0)
    camcy[rows(me_yc * 16, 16), :] = camsg[:, lanes(c * half, half)]
    cy_cam = yc_copies(camsg, camcy, 4, half, lambda yy, cc: cc)
    for cp, _, _ in cy_cam:
        cp.start()
    n0 = normalize(slots_init[...]).astype(BF)
    z_b0 = start_z(0, cy_b0)
    for cp, _, _ in cy_cam:
        cp.wait()
    camf[rows(z * 64 + quarter * 16, 16), lanes(c * half, half)] = compact(camcy[...], 8, quarter * 16, 16)

    def cam_piece(zz):
        return camf.at[rows(zz * 64 + quarter * 16, 16), lanes(c * half, half)]

    z_cam = [
        send(cam_piece(z), cam_piece(z), z_s.at[4, d], z_r.at[4, d], z=lax.rem(z + d, NZ))
        for d in range(1, NZ)
    ]
    cy_b1 = start_bundle(1)
    cy_b2 = start_bundle(2)
    for _ in ring_steps([(0, z_b0)]):
        pass
    z_b1 = start_z(1, cy_b1)
    z_b2 = start_z(2, cy_b2)
    x_cam = forward_x(4, cam_piece(z), 0)
    for d in range(1, NZ):
        z_cam[d - 1].wait()
        x_cam += forward_x(4, cam_piece(lax.rem(z - d + NZ, NZ)), d)
    ring = ring_steps([(1, z_b1), (2, z_b2)])
    next(ring)
    c_b0 = swap_core(0, (out[0], sent[0]))
    next(ring)
    done(x_cam)
    cam_half = camf.at[:, lanes(c * half, half)]
    done([send(cam_half, cam_half, c_s.at[4, 0], c_r.at[4, 0], c=1 - c)])

    def lookup(view):
        v = lax.broadcasted_iota(jnp.int32, (camf.shape[0], view.shape[1]), 0)
        return dot(onehot(v == view[...]), camf[...], 0, 0)

    px[...] = normalize(patches[...].astype(F32) + lookup(pview)).astype(BF)
    next(ring)
    cy_b3 = start_bundle(3)
    done(c_b0)

    def slot_projection(normed):
        query = (dot(normed, f0[:, 0:width]) * scale).astype(BF)
        return dot(query, f0[:, width : 2 * width], 1, 1).astype(BF)

    group = c * NX + x
    mine = pl.ds(pl.multiple_of(group * 8, 8), 8)
    state[...] = slots_init[mine, :]
    proj = slot_projection(n0)
    x_b3, c_b3 = [], []
    gaps = ((0, 1, 2, 3), (4, 5, 6, 7), ())

    def group_rows(buf, t):
        return jnp.concatenate([buf[t, g].astype(F32) for g in range(8)], axis=0)

    def share(t, value):
        psend[t] = value
        precv[t, group] = value
        return [
            send(psend.at[t], precv.at[t, group], it_s.at[t, 24 + k], it_r.at[t, 24 + k],
                 c=flip(dc), x=lax.rem(x + dx, NX))
            for k, (dc, dx) in enumerate(cx_peers())
        ]

    for t in range(ITERS):
        attn = softmax0(dot(proj, px[...], 1, 1)) + ATTN_FLOOR
        total = dot(attn.astype(BF), px[...])
        denom = jnp.sum(attn, axis=1, keepdims=True)
        for g in range(8):
            tsend[t, g, :, 0:width] = total[8 * g : 8 * g + 8].astype(BF)
            tsend[t, g, :, width : width + 128] = jnp.broadcast_to(denom[8 * g : 8 * g + 8], (8, 128)).astype(BF)
        cps = []
        for k, (dc, dx) in enumerate(cx_peers()):
            cc, xx = flip(dc), lax.rem(x + dx, NX)
            cps.append(send(tsend.at[t, cc * NX + xx], trecv.at[t, k], it_s.at[t, k], it_r.at[t, k], c=cc, x=xx))
        if t == 0:
            for _ in ring:
                pass
            z_b3 = start_z(3, cy_b3, ring=False)
        acc = tsend[t, group].astype(F32)
        for k, cp in enumerate(cps):
            cp.wait()
            acc += trecv[t, k].astype(F32)
        tysend[t] = acc.astype(BF)
        cps = [
            send(tysend.at[t], tyrecv.at[t, d], it_s.at[t, 8 + d], it_r.at[t, 8 + d], y=lax.rem(y + d, NY))
            for d in range(1, NY)
        ]
        for cp in cps:
            cp.wait()
        acc = ordered(tyrecv, tysend, t, y, NY)
        tzsend[t] = acc.astype(BF)
        cps = [
            send(tzsend.at[t], tzrecv.at[t, d], it_s.at[t, 12 + d], it_r.at[t, 12 + d], z=lax.rem(z + d, NZ))
            for d in range(1, NZ)
        ]
        if t == 0:
            c_b1 = swap_core(1, (out[1], sent[1]))
            c_b2 = swap_core(2, (out[2], sent[2]))
        if t:
            c_b3 += swap_core(3, (x_b3, []))
            x_b3 = []
        for d in gaps[t]:
            if d:
                z_b3[d - 1].wait()
            x_b3.append((d, forward_x(3, piece(3, lax.rem(z - d + NZ, NZ)), d)))
        if t == 1:
            rin[...] = rays[...].astype(F32) + lookup(rview)
            rx[...] = rin[...].astype(BF)
        if t == 2:
            done(c_b3)
            r = lax.broadcasted_iota(jnp.int32, (width, 1), 0)
            hid = 2 * r - r % 12
            unit = lax.broadcasted_iota(jnp.int32, (width, 2 * width), 1)
            ro[...] = (
                dot(f3[:, 3 * width : 3 * width + 128], onehot(unit == hid), 0, 0)
                + dot(f3[:, 3 * width + 128 : 3 * width + 256], onehot(unit == hid + 12), 0, 0)
            )[0:8].astype(BF)
        for cp in cps:
            cp.wait()
        acc = ordered(tzrecv, tzsend, t, z, NZ)
        if t == 0:
            done(c_b1)
            done(c_b2)
        mean_x = (acc[:, 0:width] / acc[:, width : width + 1]).astype(BF)
        update = dot(mean_x, f1[:, 0:width]).astype(BF)
        slots = state[...]
        a = dot(update, f2[:, 0 : 3 * width])
        b = dot(slots.astype(BF), f2[:, 3 * width : 6 * width])
        reset = jax.nn.sigmoid(a[:, 0:width] + b[:, 0:width])
        blend = jax.nn.sigmoid(a[:, width : 2 * width] + b[:, width : 2 * width])
        cand = jnp.tanh(a[:, 2 * width :] + reset * b[:, 2 * width :])
        slots = (1.0 - blend) * cand + blend * slots
        state[...] = slots
        if t + 1 < ITERS:
            cps = share(t, slot_projection(normalize(slots).astype(BF)))
            done(cps)
            proj = group_rows(precv, t).astype(BF)

    t = ITERS - 1
    ssend[...] = slots
    srecv[mine, :] = slots
    s_cps = [
        send(ssend, srecv.at[mine], gr_s.at[0, k], gr_r.at[0, k], c=flip(dc), x=lax.rem(x + dx, NX))
        for k, (dc, dx) in enumerate(cx_peers())
    ]
    slot_keys = dot(slots.astype(BF), f1[:, width : 2 * width]).astype(BF)
    r_cps = share(t, (dot(slot_keys, f3[:, 0:width], 1, 1) * scale).astype(BF))
    done(s_cps)
    done(r_cps)
    slots_all = srecv[...]
    slots_out[...] = slots_all
    low = slots_all.astype(BF)
    mix = softmax0(dot(group_rows(precv, t).astype(BF), rx[...], 1, 1)).astype(BF)
    joined = (dot(mix, low, 0, 0) + rin[...]).astype(BF)
    pre = dot(joined, f3[:, width : 3 * width])
    sig = jax.nn.sigmoid(pre)
    hidden = (pre * sig).astype(BF)
    colour = dot(ro[...], hidden, 1, 1)[0:3]
    colour_out[...] = colour
    error = colour - targets[...]
    rays_total = rin.shape[0] * NZ * NY * NC * NX
    dcol8[...] = jnp.zeros_like(dcol8)
    dcol8[0:3, :] = error * (2.0 / jnp.sqrt(jnp.float32(3.0 * rays_total)))
    dcol = dcol8[...].astype(BF)
    dpre = (dot(dcol, ro[...], 0, 0) * (sig + pre * sig * (1.0 - sig))).astype(BF)
    gro = dot(dcol, hidden)
    squared = jnp.sum(jnp.sum(error * error, axis=1, keepdims=True), axis=0, keepdims=True)

    turned = jnp.transpose(joined.astype(F32)).astype(BF)
    for zz in range(NZ):
        for h in range(NC):
            jt[384 * h + 48 * zz : 384 * h + 48 * zz + 48, :] = turned[96 * zz + 48 * h : 96 * zz + 48 * h + 48]
    order = (4, 3, 5, 2, 6, 1, 7, 0)

    def block(d):
        return rows(lax.rem(z + d, NZ) * 48, 48)

    gcs[...] = dot(jt[rows(384 * (1 - c), 384), :], dpre).astype(BF)
    g_c = {d: send(gcs.at[block(d)], gcr.at[block(d)], gc_s.at[d], gc_r.at[d], c=1 - c) for d in order}
    small[...] = jnp.zeros_like(small)
    small[0:3, :] = gro[0:3, 0:width]
    small[3:6, :] = gro[0:3, width:]
    small[6:7, :] = jnp.broadcast_to(squared, (1, width))
    sm_cps = [
        send(small, smrecv_cx.at[group], gr_s.at[2, k], gr_r.at[2, k], c=flip(dc), x=lax.rem(x + dx, NX))
        for k, (dc, dx) in enumerate(cx_peers())
    ]
    smrecv_cx[group] = small[...]
    gown[...] = dot(jt[rows(384 * c, 384), :], dpre)
    qw = 2 * width // NX
    gx = {}
    for d in order:
        g_c[d].wait()
        gsum = gown[block(d), :] + gcr[block(d), :].astype(F32)
        gown[block(d), :] = gsum
        gxs[block(d), :] = gsum.astype(BF)
        gx[d] = [
            send(gxs.at[block(d), lanes(lax.rem(quarter + k, NX) * qw, qw)], gxr.at[k, block(d)],
                 gx_s.at[k, d], gx_r.at[k, d], **along(k))
            for k in range(1, NX)
        ]
    done(sm_cps)
    acc_s = sum_of(smrecv_cx, 8)
    smy[...] = acc_s
    smrecv_y[y] = acc_s
    sm_cps = [
        send(smy, smrecv_y.at[y], gr_s.at[4, d], gr_r.at[4, d], y=lax.rem(y + d, NY)) for d in range(1, NY)
    ]
    gz = []
    for d in order:
        done(gx[d])
        acc_g = gown[block(d), lanes(quarter * qw, qw)]
        for k in range(1, NX):
            acc_g += gxr[k, block(d), :].astype(F32)
        gzs[block(d), :] = acc_g.astype(BF)
        if d:
            gz.append((d, send(gzs.at[block(d)], gzr.at[d], gr_s.at[6, d], gr_r.at[6, d], z=lax.rem(z + d, NZ))))
    done(sm_cps)
    acc_s = sum_of(smrecv_y, NY)
    smz[...] = acc_s
    smrecv_z[z] = acc_s
    sm_cps = [
        send(smz, smrecv_z.at[z], gr_s.at[5, d], gr_r.at[5, d], z=lax.rem(z + d, NZ)) for d in range(1, NZ)
    ]
    for d, cp in gz:
        cp.wait()
        acc_g += gzr[d].astype(F32)
    gys[0] = acc_g.astype(BF)
    g_b = [send(gys.at[0], gyr.at[0, d], gr_s.at[7, d], gr_r.at[7, d], **across(d)) for d in range(1, NY)]
    done(sm_cps)
    acc_s = sum_of(smrecv_z, NZ)
    gro_out[:, 0:width] = acc_s[0:3]
    gro_out[:, width:] = acc_s[3:6]
    loss_out[...] = acc_s[6:7, 0:1] / (3.0 * rays_total)
    done(g_b)
    place = x * c + y * (1 - c)
    gfs[...] = ordered(gyr, gys, 0, place, NY)

    def final(k, row, slot, **where):
        return pltpu.make_async_remote_copy(
            src_ref=gfs.at[pl.ds(pl.multiple_of(row * 24, 8), 24)], dst_ref=gfr.at[slot],
            send_sem=gr_s.at[8, k], recv_sem=gr_r.at[8, slot],
            device_id=where, device_id_type=pl.DeviceIdType.MESH,
        )

    low_half = y // 2 == 0
    keeps = y // 2 == c
    own_row = lax.rem(y, 2)

    @pl.when(keeps)
    def _():
        gfr[quarter] = gfs[pl.ds(pl.multiple_of(own_row * 24, 8), 24), :]

    def to_x(act):
        for k, (dc, dx) in enumerate(cx_peers()):
            act(final(k, own_row, quarter, c=flip(dc), x=lax.rem(x + dx, NX)))

    def to_y(act):
        for k in range(4):
            yy, cc = 2 + k // 2, k % 2

            @pl.when(jnp.logical_not((y == yy) & (c == cc)))
            def _():
                act(final(k, k // 2, quarter, y=yy, c=cc))

    @pl.when((c == 0) & low_half)
    def _():
        to_x(lambda cp: cp.start())

    @pl.when(c == 1)
    def _():
        to_y(lambda cp: cp.start())

    for slot in range(NX):
        @pl.when(jnp.logical_not(keeps & (quarter == slot)))
        def _():
            final(0, 0, slot, c=1 - c).wait_recv()

        blk = gfr[slot]
        gin_out[:, qw * slot : qw * slot + qw] = jnp.where(c == 0, blk[0:12], blk[12:24])

    @pl.when((c == 0) & low_half)
    def _():
        to_x(lambda cp: cp.wait_send())

    @pl.when(c == 1)
    def _():
        to_y(lambda cp: cp.wait_send())


def sum_of(buf, n):
    acc = buf[0]
    for j in range(1, n):
        acc += buf[j]
    return acc


def ordered(recv, own, t, me, n):
    acc = None
    for j in range(n):
        d = lax.rem(me - j + n, n)
        val = jnp.where(d == 0, own[t].astype(F32), recv[t, d].astype(F32))
        acc = val if acc is None else acc + val
    return acc


def on_device(
    patches, patch_view, rays, ray_view, targets, camera, slots_init, key_weight, value_weight,
    query_weight, gru_input, gru_hidden, mix_query, mix_key, render_in, render_out,
):
    n, width = patches.shape
    V, S = pltpu.VMEM, pltpu.SemaphoreType.DMA
    vm = pl.BlockSpec(memory_space=pltpu.VMEM)
    scratch = (
        [V((128, L // NX), BF) for L in LEN]
        + [V((width, L), BF) for L in LEN]
        + [V((16, L), BF) for L in LEN]
        + [
            V((128, 24), F32), V((16, width), BF), V((128, width // 2), BF), V((512, width), BF),
            V((n, width), BF), V((n, width), F32), V((n, width), BF), V((8, 2 * width), BF), V((8, width), F32),
            V((3, 8, 8, width + 128), BF), V((3, 8, 8, width + 128), BF),
            V((3, 8, width + 128), BF), V((3, NY, 8, width + 128), BF),
            V((3, 8, width + 128), BF), V((3, NZ, 8, width + 128), BF),
            V((3, 8, width), BF), V((3, 8, 8, width), BF), V((8, width), F32), V((64, width), F32),
            V((8, n), F32), V((8, width), F32), V((8, 8, width), F32), V((NY, 8, width), F32), V((NZ, 8, width), F32),
            V((8, width), F32), V((8, width), F32),
            V((width, n), BF), V((384, 2 * width), F32), V((384, 2 * width), BF), V((384, 2 * width), BF),
            V((384, 2 * width), BF), V((NX, 384, width // 2), BF), V((384, width // 2), BF), V((NZ, 48, width // 2), BF),
            V((1, 48, width // 2), BF), V((1, NY, 48, width // 2), BF), V((48, width // 2), F32), V((NX, 24, width // 2), F32),
            S((5, 7)), S((5, 7)), S((5, 8)), S((5, 8)), S((5, 4, 8)), S((5, 4, 8)), S((5, 8)), S((5, 8)),
            S((3, 32)), S((3, 32)), S((9, 8)), S((9, 8)), S((8,)), S((8,)), S((4, 8)), S((4, 8)),
        ]
    )
    out = pl.pallas_call(
        kernel,
        out_shape=[
            jax.ShapeDtypeStruct((64, width), F32),
            jax.ShapeDtypeStruct((3, n), F32),
            jax.ShapeDtypeStruct((1, 1), F32),
            jax.ShapeDtypeStruct((12, 2 * width), F32),
            jax.ShapeDtypeStruct((3, 2 * width), F32),
        ],
        in_specs=[vm] * 16,
        out_specs=[vm] * 5,
        scratch_shapes=scratch,
        compiler_params=pltpu.CompilerParams(collective_id=0, has_side_effects=True, vmem_limit_bytes=60 << 20),
    )(
        patch_view[None], ray_view[None], patches, rays, targets, slots_init, camera, query_weight, key_weight,
        value_weight, mix_key, gru_input, gru_hidden, mix_query, render_in, render_out,
    )
    slots, colour, loss, gin, gro = out
    return slots, colour, loss[0, 0], gin, gro


def solution(mesh):
    torus = Mesh(mesh.devices.reshape(NZ, NY, NC, NX), ("z", "y", "c", "x"))
    tok, every = ("z", "y", "c"), ("z", "y", "c", "x")
    w = P(tok, None)
    return jax.shard_map(
        on_device,
        mesh=torus,
        in_specs=(
            P(every, None), P(every), P(every, None), P(every), P(None, every), w, P(),
            w, w, w, w, w, w, w, w, P(None, tok),
        ),
        out_specs=(P(), P(None, every), P(), w, P()),
        check_vma=False,
    )
```
